128 devices in a mesh: by: 8 (over z, core), bx: 16 (over x, y).
Axes of the slice: x: 4, y: 4, z: 4, core: 2. Of those that a mesh axis runs over, the one named last changes fastest.
Arguments:
- tracers: float32 [20, 512, 16, 2048], P(None, ('by', 'bx')), may hold values from 0 to 1
- vertical_speed: float32 [20, 512, 2048], P(None, ('by', 'bx')), may hold values from -0.4 to 0.4
- diffusivity: float32 [20, 512, 2048], P(None, ('by', 'bx')), may hold values from 0.02 to 2
- buoyancy_force: bfloat16 [20, 512, 2048], P(None, ('by', 'bx')), may hold values from -2.1 to 2.1
- wet_levels: int32 [512, 2048], P(('by', 'bx')), may hold values from 0 to 20
- surface_patch: int32 [512, 2048], P(('by', 'bx')), may hold values from 0 to 15
- prior_height: float32 [512, 2048], P(('by', 'bx')), may hold values from -5 to 5
- land_mask: int32 [512, 16, 128], P(('by', 'bx')), may hold values 0 or 1
- baroclinic_map: int32 [512], replicated, may hold values from 0 to 511, as said below
- barotropic_map: int32 [512], replicated, may hold values from 0 to 511, as said below
Outputs:
- new_tracers: float32 [20, 512, 16, 2048], P(None, ('by', 'bx'))
- surface_height: float32 [512, 16, 128], P(('by', 'bx'))
The draws below stay inside these ranges and needn't reach their ends.
Inputs may be any that keep to these rules, and one draw needn't show every extreme that they name: baroclinic_map[s] is the geographic block held in baroclinic slot s, blocks numbered row by row with 64 to a block row; it lies in block row s // 64, and every block appears once. barotropic_map[s] is the geographic block held in barotropic slot s, blocks numbered row by row with 64 to a block row; it lies in block row s // 64, and every block appears once.
All inputs are finite; a program needn't handle non-finite values. No bound on the sum of `land_mask` on one device may be relied on, other than what follows from the above.
Results may differ from the reference program's by a relative error of at most 0.0003.
Values sent between devices are 32-bit elements; how exact they have to be, the bound alone decides.
A program may use at most 128 MiB of HBM per device.

```python
import math
import jax
import jax.numpy as jnp
from jax import lax

BH = 16
BW = 128
LEV = 20
TR = 16
ITERS = 6
GBX = 64
NB = 512
CELLS = 2048
N_BY = 8


def band_permutation(key):
    band_count = NB // GBX
    scores = jax.random.randint(key, (band_count, GBX), 0, 1 << 20) * GBX + jnp.arange(GBX, dtype=jnp.int32)[None, :]
    ordering = jnp.argsort(scores, axis=1, stable=True).astype(jnp.int32)
    offsets = (jnp.arange(band_count, dtype=jnp.int32) * GBX)[:, None]
    return (ordering + offsets).reshape(NB).astype(jnp.int32)


def draw_baroclinic_map(key, part):
    return band_permutation(jax.random.fold_in(key, 11))


def draw_barotropic_map(key, part):
    return band_permutation(jax.random.fold_in(key, 23))


def slot_offsets(key, reach):
    return jax.random.uniform(key, (NB,), jnp.float32, -reach, reach)


def draw_prior_height(key, part):
    offsets = slot_offsets(jax.random.fold_in(key, 31), 3.0)
    base = jnp.clip(0.5 * jax.random.normal(jax.random.fold_in(key, 33), (NB, CELLS), jnp.float32), -2.0, 2.0)
    return (base + offsets[:, None]).astype(jnp.float32)


def draw_buoyancy_force(key, part):
    offsets = slot_offsets(jax.random.fold_in(key, 41), 0.3)
    base = jnp.clip(0.3 * jax.random.normal(jax.random.fold_in(key, 43), (LEV, NB, CELLS), jnp.float32), -1.8, 1.8)
    level_index = lax.broadcasted_iota(jnp.int32, (LEV, 1, 1), 0)
    top_level = (level_index == 0).astype(jnp.float32)
    return (base + top_level * offsets[None, :, None]).astype(jnp.bfloat16)


def plant(drawn, rng, least, high):
    extent = drawn.shape
    index_at = [jax.random.randint(jax.random.fold_in(rng, axis), (), 0, extent[axis]) for axis in range(len(extent))]
    drawn = drawn.at[tuple(index_at)].set(least)
    longest = extent.index(max(extent))
    index_at[longest] = (index_at[longest] + 1) % extent[longest]
    return drawn.at[tuple(index_at)].set(high)


def shard_levels(rng, dims, cuts, least, high):
    def one(position, shards_of):
        steps = jax.random.uniform(jax.random.fold_in(jax.random.fold_in(rng, 6), position), (shards_of,), jnp.float32, least / len(cuts), high / len(cuts))
        return jnp.repeat(jnp.exp(steps), dims[position] // shards_of).reshape((-1,) + (1,) * (len(dims) - position - 1))

    level = one(*cuts[0])
    for cut in cuts[1:]:
        level = level * one(*cut)
    return level


def setup_inputs(seed: int = 0) -> dict:
    key_list = jax.random.split(jax.random.key(seed), 11)
    return {
        "tracers": jnp.clip(1.0 * jax.random.uniform(key_list[0], (LEV, NB, TR, CELLS), jnp.float32) ** shard_levels(key_list[0], (LEV, NB, TR, CELLS), ((1, 128),), -0.2, 0.2), 0.0, 1.0),
        "vertical_speed": jnp.clip(jax.random.uniform(key_list[1], (LEV, NB, CELLS), jnp.float32, -0.4, 0.4) * shard_levels(key_list[1], (LEV, NB, CELLS), ((1, 128),), -0.4, 0.0), -0.4, 0.4),
        "diffusivity": jnp.clip(jnp.exp(math.log(2.0) - 4.6051702 * jax.random.uniform(key_list[2], (LEV, NB, CELLS), jnp.float32) ** shard_levels(key_list[2], (LEV, NB, CELLS), ((1, 128),), -0.2, 0.2)), 0.02, 2.0),
        "buoyancy_force": draw_buoyancy_force(jax.random.fold_in(key_list[10], 71), 0),
        "wet_levels": plant(jax.random.randint(key_list[4], (NB, CELLS), 0, LEV + 1), jax.random.fold_in(key_list[4], 1), 0, LEV).astype(jnp.int32),
        "surface_patch": plant(jax.random.randint(key_list[5], (NB, CELLS), 0, TR), jax.random.fold_in(key_list[5], 1), 0, TR - 1).astype(jnp.int32),
        "prior_height": draw_prior_height(jax.random.fold_in(key_list[10], 71), 0),
        "land_mask": plant((jax.random.randint(key_list[7], (NB, BH, BW), 0, 8) < 7).astype(jnp.int32), jax.random.fold_in(key_list[7], 1), 0, 1),
        "baroclinic_map": draw_baroclinic_map(jax.random.fold_in(key_list[10], 71), 0),
        "barotropic_map": draw_barotropic_map(jax.random.fold_in(key_list[10], 71), 0),
    }


RESTORE = 0.5
SURFACE = 0.1
FACE_SCALE = 2.0


def column_step(tracers, vertical_speed, diffusivity, wet_levels, surface_patch):
    depth_index = lax.broadcasted_iota(jnp.int32, vertical_speed.shape, 0)
    wet_level = (depth_index < wet_levels[None]).astype(jnp.float32)
    open_faces = (depth_index + 1 < wet_levels[None]).astype(jnp.float32)
    speed_open = (vertical_speed * open_faces)[:, :, None]
    shifted_up = jnp.concatenate([tracers[1:], jnp.zeros_like(tracers[:1])], axis=0)
    flux_below = jnp.maximum(speed_open, 0.0) * shifted_up + jnp.minimum(speed_open, 0.0) * tracers
    flux_above = jnp.concatenate([jnp.zeros_like(flux_below[:1]), flux_below[:-1]], axis=0)
    advected = wet_level[:, :, None] * (tracers + flux_below - flux_above)
    mixing = diffusivity * open_faces
    mixing_above = jnp.concatenate([jnp.zeros_like(mixing[:1]), mixing[:-1]], axis=0)
    surface_row = (depth_index == 0).astype(jnp.float32) * wet_level * RESTORE
    diagonal = 1.0 + mixing + mixing_above + surface_row
    tracer_ids = lax.broadcasted_iota(jnp.int32, (1, tracers.shape[2], 1), 1)
    targets = (surface_patch[:, None, :] == tracer_ids).astype(jnp.float32)
    right_side = advected + surface_row[:, :, None] * targets[None]

    def forward(carry, layer):
        ratio_prev, value_prev = carry
        lower_band, diag_now, upper_band, right_now = layer
        pivot_now = diag_now - lower_band * ratio_prev
        ratio_now = upper_band / pivot_now
        value_now = (right_now - lower_band[:, None] * value_prev) / pivot_now[:, None]
        return (ratio_now, value_now), (ratio_now, value_now)

    start_carry = (jnp.zeros(mixing.shape[1:], jnp.float32), jnp.zeros(tracers.shape[1:], jnp.float32))
    ignored, (ratios, values) = lax.scan(forward, start_carry, (-mixing_above, diagonal, -mixing, right_side))

    def backward(following, layer):
        ratio_now, value_now = layer
        solved_now = value_now - ratio_now[:, None] * following
        return solved_now, solved_now

    ignored_too, solved = lax.scan(backward, jnp.zeros(tracers.shape[1:], jnp.float32), (ratios, values), reverse=True)
    return solved


def to_grid(blocks_flat, block_map):
    shaped = blocks_flat.reshape(NB, BH, BW)
    ordered = jnp.zeros_like(shaped).at[block_map].set(shaped)
    return ordered.reshape(N_BY, GBX, BH, BW).transpose(0, 2, 1, 3).reshape(N_BY * BH, GBX * BW)


def from_grid(grid, block_map):
    ordered = grid.reshape(N_BY, BH, GBX, BW).transpose(0, 2, 1, 3).reshape(NB, BH, BW)
    return ordered[block_map]


def next_rows(grid):
    return jnp.concatenate([grid[1:], jnp.zeros_like(grid[:1])], axis=0)


def prev_rows(grid):
    return jnp.concatenate([jnp.zeros_like(grid[:1]), grid[:-1]], axis=0)


def reference(tracers, vertical_speed, diffusivity, buoyancy_force, wet_levels, surface_patch, prior_height, land_mask, baroclinic_map, barotropic_map):
    def one_slot(column_items):
        slot_tracers, slot_speed, slot_mixing, slot_wet, slot_patch = column_items
        stepped = column_step(slot_tracers[:, None], slot_speed[:, None], slot_mixing[:, None], slot_wet[None], slot_patch[None])
        return stepped[:, 0]

    stepped_all = lax.map(one_slot, (jnp.moveaxis(tracers, 1, 0), jnp.moveaxis(vertical_speed, 1, 0), jnp.moveaxis(diffusivity, 1, 0), wet_levels, surface_patch))
    new_tracers = jnp.moveaxis(stepped_all, 0, 1)

    depth_index = lax.broadcasted_iota(jnp.int32, buoyancy_force.shape, 0)
    wet_level = (depth_index < wet_levels[None]).astype(jnp.float32)
    forcing = jnp.sum(wet_level * buoyancy_force.astype(jnp.float32), axis=0)
    forcing_grid = to_grid(forcing, baroclinic_map)
    depth_grid = to_grid(wet_levels.astype(jnp.float32), baroclinic_map)
    prior_grid = to_grid(prior_height, baroclinic_map)
    ocean_grid = to_grid(land_mask.astype(jnp.float32), barotropic_map)

    face_factor = FACE_SCALE / LEV
    east_face = face_factor * jnp.minimum(depth_grid, jnp.roll(depth_grid, -1, axis=1)) * ocean_grid * jnp.roll(ocean_grid, -1, axis=1)
    west_face = jnp.roll(east_face, 1, axis=1)
    south_face = face_factor * jnp.minimum(depth_grid, next_rows(depth_grid)) * ocean_grid * next_rows(ocean_grid)
    north_face = prev_rows(south_face)
    centre_weight = SURFACE * ocean_grid + (1.0 - ocean_grid)
    precond_diagonal = centre_weight + east_face + west_face + south_face + north_face

    def operate(field_grid):
        centre = centre_weight * field_grid
        result = centre + east_face * (field_grid - jnp.roll(field_grid, -1, axis=1))
        result = result + west_face * (field_grid - jnp.roll(field_grid, 1, axis=1))
        result = result + south_face * (field_grid - next_rows(field_grid))
        return result + north_face * (field_grid - prev_rows(field_grid))

    solution = ocean_grid * prior_grid
    residual = ocean_grid * forcing_grid - operate(solution)
    precond = residual / precond_diagonal
    direction = precond
    norm_now = jnp.sum(residual * precond)
    for step_index in range(ITERS):
        image_field = operate(direction)
        step_size = norm_now / jnp.sum(direction * image_field)
        solution = solution + step_size * direction
        residual = residual - step_size * image_field
        precond = residual / precond_diagonal
        norm_next = jnp.sum(residual * precond)
        direction = precond + (norm_next / norm_now) * direction
        norm_now = norm_next
    surface_height = from_grid(solution, barotropic_map)
    return new_tracers, surface_height
```

```python
import jax
import jax.numpy as jnp
from jax import lax
from jax.experimental import pallas as pl
from jax.experimental.pallas import tpu as pltpu
from jax.sharding import PartitionSpec as P

MESH = pl.DeviceIdType.MESH
ITERS = 6
RESTORE = 0.5
SURFACE = 0.1
FACE_SCALE = 2.0
LEV, TR, BH, BW = 20, 16, 16, 128
GBX, BLOCKS, NBX, NBY = 64, 4, 16, 8
LANES = 256
FACE = FACE_SCALE / LEV
SHIFTS = (0.0, 2.0, 1.0, 1.577, 0.4226, 0.1)
ALPHA_MAX = 82.0
PAIRS = [(i, j) for i in range(ITERS) for j in range(i, ITERS + 1)]


def columns_kernel(tr_ref, speed_ref, diff_ref, wet_ref, patch_ref, out_ref, coef):
    lanes = tr_ref.shape[3]
    wet = wet_ref[...]
    zero = jnp.zeros(wet.shape, jnp.float32)
    mix_above, pos_above, neg_above, ratio_above = zero, zero, zero, zero
    for k in range(LEV):
        is_wet = (wet > k).astype(jnp.float32)
        is_open = (wet > k + 1).astype(jnp.float32)
        speed = speed_ref[k] * is_open
        pos, neg = jnp.maximum(speed, 0.0), jnp.minimum(speed, 0.0)
        mix = diff_ref[k] * is_open
        pivot = 1.0 + mix + mix_above
        if k == 0:
            pivot = pivot + RESTORE * is_wet
        pivot = pivot - mix_above * ratio_above
        inv = 1.0 / pivot
        scale = is_wet * inv
        coef[0, k] = scale * (1.0 + neg - pos_above)
        coef[1, k] = scale * pos
        coef[2, k] = -scale * neg_above
        coef[3, k] = mix_above * inv
        ratio = mix * inv
        coef[4, k] = ratio
        if k == 0:
            coef[5, 0] = RESTORE * scale
        mix_above, pos_above, neg_above, ratio_above = mix, pos, neg, ratio
    ids = lax.broadcasted_iota(jnp.int32, (TR, 128), 0)
    for n in range(BLOCKS):
        for l in range(lanes // 128):
            sl = pl.ds(l * 128, 128)

            def c(i, k):
                return coef[i, k, pl.ds(n, 1), sl]

            values = []
            above, here, value = None, tr_ref[0, n, :, sl], None
            for k in range(LEV):
                new = c(0, k) * here
                if k + 1 < LEV:
                    below = tr_ref[k + 1, n, :, sl]
                    new = new + c(1, k) * below
                if k == 0:
                    target = patch_ref[pl.ds(n, 1), sl] == ids
                    new = new + jnp.where(target, c(5, 0), 0.0)
                else:
                    new = new + c(2, k) * above + c(3, k) * value
                value = new
                values.append(value)
                above, here = here, below
            follow = values[-1]
            out_ref[LEV - 1, n, :, sl] = follow
            for k in range(LEV - 2, -1, -1):
                follow = values[k] + c(4, k) * follow
                out_ref[k, n, :, sl] = follow


def column_step(tracers, speed, diff, wet, patch):
    lanes = 256
    cells = wet.shape[1]
    big = pl.BlockSpec((LEV, BLOCKS, TR, lanes), lambda i: (0, 0, 0, i))
    mid = pl.BlockSpec((LEV, BLOCKS, lanes), lambda i: (0, 0, i))
    low = pl.BlockSpec((BLOCKS, lanes), lambda i: (0, i))
    return pl.pallas_call(
        columns_kernel,
        grid=(cells // lanes,),
        in_specs=[big, mid, mid, low, low],
        out_specs=big,
        out_shape=jax.ShapeDtypeStruct(tracers.shape, jnp.float32),
        scratch_shapes=[pltpu.VMEM((6, LEV, BLOCKS, lanes), jnp.float32)],
        compiler_params=pltpu.CompilerParams(dimension_semantics=("arbitrary",)),
        name="columns",
    )(tracers, speed, diff, wet, patch)


def table_index(kind, role, slot, side):
    return ((kind * 3 + role) * BLOCKS + slot) * 3 + side


def barotropic_kernel(
    tab, buoy_ref, wet_ref, prior_ref, land_ref, out_ref,
    gat, nsend, nrecv, basis, gram, ring_a, ring_b, ssem, rsem,
):
    row = lax.axis_index("by")
    me = lax.axis_index("bx")
    core = lax.rem(row, 2)
    step_a = 4 - 3 * core
    step_b = 1 + 3 * core
    px, py = me // 4, lax.rem(me, 4)
    a = px + core * (py - px)
    b = py + core * (px - py)

    def dev(i, j):
        return lax.rem(a + i, 4) * step_a + lax.rem(b + j, 4) * step_b

    barrier = pltpu.get_barrier_semaphore()
    for i in range(1, NBX):
        pl.semaphore_signal(
            barrier, inc=1, device_id={"bx": lax.rem(me + i, NBX)}, device_id_type=MESH
        )
    for i in range(1, NBY):
        pl.semaphore_signal(
            barrier, inc=1, device_id={"by": lax.rem(row + i, NBY)}, device_id_type=MESH
        )

    mine = me * BLOCKS
    wet = wet_ref[...]
    total = jnp.zeros(wet.shape, jnp.float32)
    for k in range(LEV):
        total = total + jnp.where(wet > k, buoy_ref[k].astype(jnp.float32), 0.0)
    fields = (total, wet.astype(jnp.float32), prior_ref[...])
    for q in range(3):
        for n in range(BLOCKS):
            for r in range(BH):
                gat[mine + n, q, pl.ds(r, 1), :] = fields[q][n : n + 1, r * BW : (r + 1) * BW]
    for n in range(BLOCKS):
        gat[mine + n, 3] = land_ref[n].astype(jnp.float32)

    pl.semaphore_wait(barrier, NBX - 1 + NBY - 1)

    copies = {}

    def send(tag, where, start, count, to):
        piece = gat.at[pl.ds(where * BLOCKS + start, count)]
        copies[tag] = pltpu.make_async_remote_copy(
            src_ref=piece,
            dst_ref=piece,
            send_sem=ssem.at[tag],
            recv_sem=rsem.at[tag],
            device_id={"bx": to},
            device_id_type=MESH,
        )
        copies[tag].start()

    def arrived(tag):
        copies[tag].wait_recv()

    half = BLOCKS // 2
    send(0, me, 0, BLOCKS, dev(1, 0))
    send(1, me, 0, BLOCKS, dev(3, 0))
    send(4, me, 0, BLOCKS, dev(0, 1))
    send(5, me, 0, BLOCKS, dev(0, 3))
    arrived(0)
    send(2, dev(3, 0), 0, half, dev(1, 0))
    send(8, dev(3, 0), 0, BLOCKS, dev(0, 1))
    send(9, dev(3, 0), 0, BLOCKS, dev(0, 3))
    arrived(1)
    send(3, dev(1, 0), half, half, dev(3, 0))
    send(12, dev(1, 0), 0, BLOCKS, dev(0, 1))
    send(13, dev(1, 0), 0, BLOCKS, dev(0, 3))

    def relay(t, i):
        arrived(4 + 4 * t)
        send(6 + 4 * t, dev(i, 3), 0, half, dev(0, 1))
        arrived(5 + 4 * t)
        send(7 + 4 * t, dev(i, 1), half, half, dev(0, 3))

    relay(0, 0)
    arrived(2)
    arrived(3)
    send(16, dev(2, 0), 0, BLOCKS, dev(0, 1))
    send(17, dev(2, 0), 0, BLOCKS, dev(0, 3))
    relay(1, 3)
    relay(2, 1)
    relay(3, 2)
    for t in range(4):
        arrived(6 + 4 * t)
        arrived(7 + 4 * t)
    for tag in range(20):
        copies[tag].wait_send()

    west_half = lax.broadcasted_iota(jnp.int32, (8, BW), 1) >= BW // 2

    def piece(role, n, q, side, rows):
        kind = 1 if q == 3 else 0
        return gat[tab[table_index(kind, role, n, side)], q, rows, :]

    def extended(role, n, q, rows):
        middle = piece(role, n, q, 1, rows)
        beside = jnp.where(west_half, piece(role, n, q, 0, rows), piece(role, n, q, 2, rows))
        return middle, beside

    for role, rows in ((1, pl.ds(BH - 8, 8)), (2, pl.ds(0, 8))):
        for n in range(BLOCKS):
            for q in range(4):
                middle, beside = extended(role, n, q, rows)
                nsend[role - 1, n, q, :, pl.ds(0, BW)] = middle
                nsend[role - 1, n, q, :, pl.ds(BW, BW)] = beside
    halo = []
    for d in range(2):
        to = lax.rem(row + (1 if d == 0 else NBY - 1), NBY)
        copy = pltpu.make_async_remote_copy(
            src_ref=nsend.at[d],
            dst_ref=nrecv.at[d],
            send_sem=ssem.at[20 + d],
            recv_sem=rsem.at[20 + d],
            device_id={"by": to},
            device_id_type=MESH,
        )
        copy.start()
        halo.append(copy)
    for copy in halo:
        copy.wait()

    has_north = (row > 0).astype(jnp.float32)
    has_south = (row < NBY - 1).astype(jnp.float32)
    acc = [None] * len(PAIRS)
    for n in range(BLOCKS):
        whole = []
        for q in range(4):
            north, south = nrecv[0, n, q], nrecv[1, n, q]
            if q == 3:
                north, south = north * has_north, south * has_south
            parts = [north]
            for r in range(0, BH, 8):
                middle, beside = extended(0, n, q, pl.ds(r, 8))
                parts.append(jnp.concatenate([middle, beside], axis=1))
            parts.append(south)
            whole.append(jnp.concatenate(parts, axis=0))
        force, depth, prior, ocean = whole
        rows = BH + 16

        def east(v):
            return pltpu.roll(v, LANES - 1, 1)

        def west(v):
            return pltpu.roll(v, 1, 1)

        def south_of(v):
            return pltpu.roll(v, rows - 1, 0)

        def north_of(v):
            return pltpu.roll(v, 1, 0)

        face_e = FACE * jnp.minimum(depth, east(depth)) * ocean * east(ocean)
        face_s = FACE * jnp.minimum(depth, south_of(depth)) * ocean * south_of(ocean)
        face_w, face_n = west(face_e), north_of(face_s)
        centre = SURFACE * ocean + (1.0 - ocean)
        diag = centre + face_e + face_w + face_s + face_n
        inv = 1.0 / diag
        centre, face_e, face_w = centre * inv, face_e * inv, face_w * inv
        face_s, face_n = face_s * inv, face_n * inv

        def scaled(v):
            out = centre * v + face_e * (v - east(v)) + face_w * (v - west(v))
            return out + face_s * (v - south_of(v)) + face_n * (v - north_of(v))

        def own(v):
            return v[8 : 8 + BH, :BW]

        guess = ocean * prior
        u = ocean * force * inv - scaled(guess)
        weight = own(diag)
        basis[n, ITERS] = own(guess)
        mine_of, weighted = [], []
        for k in range(ITERS + 1):
            mine_of.append(own(u))
            if k < ITERS:
                basis[n, k] = mine_of[k]
                weighted.append(weight * mine_of[k])
                image = scaled(u)
                u = image - SHIFTS[k] * u if SHIFTS[k] else image
        for e, (i, j) in enumerate(PAIRS):
            prod = weighted[i] * mine_of[j]
            prod = prod[:8] + prod[8:]
            acc[e] = prod if acc[e] is None else acc[e] + prod

    entries = 32
    for e in range(len(PAIRS)):
        gram[pl.ds(e, 1), :] = jnp.sum(acc[e], axis=0, keepdims=True)
    gram[pl.ds(len(PAIRS), entries - len(PAIRS)), :] = jnp.zeros(
        (entries - len(PAIRS), BW), jnp.float32
    )
    on_diag = lax.broadcasted_iota(jnp.int32, (entries, BW), 0) == lax.broadcasted_iota(
        jnp.int32, (entries, BW), 1
    )
    placed = jnp.where(on_diag, jnp.sum(gram[...], axis=1, keepdims=True), 0.0)
    packed = placed[0:8] + placed[8:16] + placed[16:24] + placed[24:32]

    def all_sum(value, ring, index, count, axis, base):
        ring[index] = value
        sent = []
        for i in range(1, count):
            copy = pltpu.make_async_remote_copy(
                src_ref=ring.at[index],
                dst_ref=ring.at[index],
                send_sem=ssem.at[base + i],
                recv_sem=rsem.at[base + i],
                device_id={axis: lax.rem(index + i, count)},
                device_id_type=MESH,
            )
            copy.start()
            sent.append(copy)
        for copy in sent:
            copy.wait()
        return jnp.sum(ring[...], axis=0)

    packed = all_sum(packed, ring_a, me, NBX, "bx", 22)
    packed = all_sum(packed, ring_b, row, NBY, "by", 22 + NBX)
    line = jnp.sum(packed, axis=0, keepdims=True)
    spread = jnp.sum(jnp.where(on_diag, line, 0.0), axis=1, keepdims=True)
    spread = jnp.broadcast_to(spread, (entries, BW))
    g = {}
    for e, (i, j) in enumerate(PAIRS):
        g[i, j] = g[j, i] = spread[e : e + 1]

    def form(left, right):
        out = None
        for i, vi in enumerate(left):
            inner = None
            for j, vj in enumerate(right):
                term = g[i, j] * vj
                inner = term if inner is None else inner + term
            out = vi * inner if out is None else out + vi * inner
        return out

    one = jnp.ones((1, BW), jnp.float32)
    zero = jnp.zeros((1, BW), jnp.float32)
    p, z = [one], [one]
    x = [zero] * ITERS
    rz = g[0, 0]
    for it in range(ITERS):
        y = [SHIFTS[k] * p[k] if SHIFTS[k] else zero for k in range(it + 1)] + [zero]
        for k in range(it + 1):
            y[k + 1] = y[k + 1] + p[k]
        pq = form(p, y)
        live = jnp.logical_and(rz > 0.0, pq > 0.0)
        alpha = jnp.where(live, rz, 0.0) / jnp.where(live, pq, 1.0)
        alpha = jnp.minimum(alpha, ALPHA_MAX)
        for k in range(it + 1):
            x[k] = x[k] + alpha * p[k]
        if it + 1 < ITERS:
            z = [zk - alpha * yk for zk, yk in zip(z + [zero], y)]
            rz_new = jnp.maximum(form(z, z), 0.0)
            beta = jnp.where(live, rz_new, 0.0) / jnp.where(live, rz, 1.0)
            p = [zk + beta * pk for zk, pk in zip(z, p + [zero])]
            rz = rz_new
    for n in range(BLOCKS):
        height = basis[n, ITERS]
        for k in range(ITERS):
            height = height + x[k] * basis[n, k]
        out_ref[n] = height


def barotropic(table, buoyancy, wet, prior, land):
    vmem = pl.BlockSpec(memory_space=pltpu.VMEM)
    tags = 22 + NBX + NBY
    return pl.pallas_call(
        barotropic_kernel,
        out_shape=jax.ShapeDtypeStruct((BLOCKS, BH, BW), jnp.float32),
        in_specs=[pl.BlockSpec(memory_space=pltpu.SMEM)] + [vmem] * 4,
        out_specs=vmem,
        scratch_shapes=[
            pltpu.VMEM((GBX, 4, BH, BW), jnp.float32),
            pltpu.VMEM((2, BLOCKS, 4, 8, LANES), jnp.float32),
            pltpu.VMEM((2, BLOCKS, 4, 8, LANES), jnp.float32),
            pltpu.VMEM((BLOCKS, ITERS + 1, BH, BW), jnp.float32),
            pltpu.VMEM((32, BW), jnp.float32),
            pltpu.VMEM((NBX, 8, BW), jnp.float32),
            pltpu.VMEM((NBY, 8, BW), jnp.float32),
            pltpu.SemaphoreType.DMA((tags,)),
            pltpu.SemaphoreType.DMA((tags,)),
        ],
        compiler_params=pltpu.CompilerParams(collective_id=0, has_side_effects=True),
        name="barotropic",
    )(table, buoyancy, wet, prior, land)


def index_table(baroclinic_map, barotropic_map):
    row, column = lax.axis_index("by"), lax.axis_index("bx")
    first = row * GBX
    clinic = lax.dynamic_slice_in_dim(baroclinic_map, first, GBX) - first
    tropic = lax.dynamic_slice_in_dim(barotropic_map, first, GBX) - first
    rows = (row + jnp.array([0, 1, NBY - 1], jnp.int32)) % NBY
    blocks = barotropic_map.reshape(NBY, NBX, BLOCKS)
    wanted = jnp.stack(
        [lax.dynamic_slice(blocks, (rows[i], column, 0), (1, 1, BLOCKS))[0, 0] for i in range(3)]
    ) % GBX
    sides = jnp.array([-1, 0, 1], jnp.int32)
    wanted = (wanted[:, :, None] + sides + GBX) % GBX
    places = jnp.arange(GBX, dtype=jnp.int32)
    held = jnp.stack([clinic, tropic])
    match = held[:, None, None, None, :] == wanted[None, :, :, :, None]
    return jnp.sum(jnp.where(match, places, 0), axis=-1).reshape(-1)


def local(
    tracers, vertical_speed, diffusivity, buoyancy_force, wet_levels, surface_patch,
    prior_height, land_mask, baroclinic_map, barotropic_map,
):
    table = index_table(baroclinic_map, barotropic_map)
    height = barotropic(table, buoyancy_force, wet_levels, prior_height, land_mask)
    new_tracers = column_step(tracers, vertical_speed, diffusivity, wet_levels, surface_patch)
    return new_tracers, height


def solution(mesh):
    return jax.shard_map(
        local,
        mesh=mesh,
        in_specs=(
            P(None, ("by", "bx"), None, None),
            P(None, ("by", "bx"), None),
            P(None, ("by", "bx"), None),
            P(None, ("by", "bx"), None),
            P(("by", "bx"), None),
            P(("by", "bx"), None),
            P(("by", "bx"), None),
            P(("by", "bx"), None, None),
            P(),
            P(),
        ),
        out_specs=(P(None, ("by", "bx"), None, None), P(("by", "bx"), None, None)),
        check_vma=False,
    )
```

```python
import jax
import jax.numpy as jnp
from jax import lax
from jax.experimental import pallas as pl
from jax.experimental.pallas import tpu as pltpu
from jax.sharding import PartitionSpec as P

MESH = pl.DeviceIdType.MESH
ITERS = 6
RESTORE = 0.5
SURFACE = 0.1
FACE_SCALE = 2.0
LEV, TR, BH, BW = 20, 16, 16, 128
CELLS = BH * BW
GBX, BLOCKS, NBX, NBY = 64, 4, 16, 8
LANES = 256
FACE = FACE_SCALE / LEV
SHIFTS = (0.0, 2.0, 1.0, 1.577, 0.4226, 0.1)
ALPHA_MAX = 82.0
PAIRS = [(i, j) for i in range(ITERS) for j in range(i, ITERS + 1)]
ENTRIES = 32
CHUNKS = 8
PARTS = (range(0, 2), range(2, 5), range(5, 8))
OWN_TILES = BLOCKS * 3 * 2 + 4
ROW_TILES = BLOCKS * 4 + 2


def columns(tile, tr, speed_ref, diff_ref, wet_ref, patch_ref, coef):
    sl = pl.ds(pl.multiple_of(tile * 128, 128), 128)
    wet = wet_ref[:, sl]
    zero = jnp.zeros(wet.shape, jnp.float32)
    mix_above, pos_above, neg_above, ratio_above = zero, zero, zero, zero
    for k in range(LEV):
        is_wet = (wet > k).astype(jnp.float32)
        is_open = (wet > k + 1).astype(jnp.float32)
        speed = speed_ref[k, :, sl] * is_open
        pos, neg = jnp.maximum(speed, 0.0), jnp.minimum(speed, 0.0)
        mix = diff_ref[k, :, sl] * is_open
        pivot = 1.0 + mix + mix_above
        if k == 0:
            pivot = pivot + RESTORE * is_wet
        pivot = pivot - mix_above * ratio_above
        inv = 1.0 / pivot
        scale = is_wet * inv
        coef[0, k] = scale * (1.0 + neg - pos_above)
        coef[1, k] = scale * pos
        coef[2, k] = -scale * neg_above
        coef[3, k] = mix_above * inv
        ratio = mix * inv
        coef[4, k] = ratio
        if k == 0:
            coef[5, 0] = RESTORE * scale
        mix_above, pos_above, neg_above, ratio_above = mix, pos, neg, ratio
    ids = lax.broadcasted_iota(jnp.int32, (TR, 128), 0)
    for n in range(BLOCKS):

        def c(i, k):
            return coef[i, k, pl.ds(n, 1), :]

        values = []
        above, here, value = None, tr[0, n, :, sl], None
        for k in range(LEV):
            new = c(0, k) * here
            if k + 1 < LEV:
                below = tr[k + 1, n, :, sl]
                new = new + c(1, k) * below
            if k == 0:
                target = patch_ref[pl.ds(n, 1), sl] == ids
                new = new + jnp.where(target, c(5, 0), 0.0)
            else:
                new = new + c(2, k) * above + c(3, k) * value
            value = new
            values.append(value)
            above, here = here, below
        follow = values[-1]
        tr[LEV - 1, n, :, sl] = follow
        for k in range(LEV - 2, -1, -1):
            follow = values[k] + c(4, k) * follow
            tr[k, n, :, sl] = follow


def step_kernel(
    cmap_hbm, tmap_hbm, buoy_hbm, wet_hbm, patch_hbm, prior_hbm, land_hbm, speed_hbm, diff_hbm, tr_hbm,
    tr, out_ref,
    cmap, tmap, buoy_ref, wet_ref, patch_ref, prior_ref, land_ref, speed_ref, diff_ref, coef,
    gat, send_own, recv_own, send_row, recv_row, basis, gram, ring_a, ring_b,
    tab_v, tab_s, lsem, tsem, ssem, rsem,
):
    row = lax.axis_index("by")
    me = lax.axis_index("bx")
    core = lax.rem(row, 2)
    below_row = lax.rem(row + 1, NBY)
    above_row = lax.rem(row + NBY - 1, NBY)
    step_a = 4 - 3 * core
    step_b = 1 + 3 * core
    px, py = me // 4, lax.rem(me, 4)
    a = px + core * (py - px)
    b = py + core * (px - py)

    def dev(i, j):
        return lax.rem(a + i, 4) * step_a + lax.rem(b + j, 4) * step_b

    barrier = pltpu.get_barrier_semaphore()

    def greet(**where):
        pl.semaphore_signal(barrier, inc=1, device_id=where, device_id_type=MESH)

    for i in range(1, NBX):
        greet(bx=lax.rem(me + i, NBX))
    for i in range(1, NBY):
        greet(by=lax.rem(row + i, NBY))
    for i in range(1, 4):
        greet(by=below_row, bx=dev(0, i))
        greet(by=above_row, bx=dev(0, i))
        greet(by=below_row, bx=dev(i, 0))
        greet(by=above_row, bx=dev(i, 0))
    greeted = NBX - 1 + NBY - 1 + 12

    local = [
        (cmap_hbm, cmap), (tmap_hbm, tmap), (buoy_hbm, buoy_ref), (wet_hbm, wet_ref), (prior_hbm, prior_ref), (land_hbm, land_ref),
        (speed_hbm, speed_ref), (diff_hbm, diff_ref), (patch_hbm, patch_ref),
    ]
    loads = [pltpu.make_async_copy(s, d, lsem.at[i]) for i, (s, d) in enumerate(local)]
    for load in loads:
        load.start()
    width = CELLS // CHUNKS
    streams = []
    for i in range(CHUNKS):
        part = (slice(None), slice(None), slice(None), pl.ds(i * width, width))
        streams.append(pltpu.make_async_copy(tr_hbm.at[part], tr.at[part], tsem.at[i]))
        streams[i].start()

    lane = lax.broadcasted_iota(jnp.int32, (1, BW), 1)
    sources = ((row, core, b), (above_row, 1 - core, a), (below_row, 1 - core, a))

    def fill(s, tabs):
        tabs = list(tabs)
        sx, sy, slot = s // 16, lax.rem(s // 4, 4), lax.rem(s, 4)
        for r, (which, its_core, its_b) in enumerate(sources):
            sa = sx + its_core * (sy - sx)
            sb = sy + its_core * (sx - sy)
            offset = lax.rem(its_b - sb + 4, 4)
            for kind, ref in enumerate((cmap, tmap)):
                hit = lane == lax.rem(ref[which * GBX + s], GBX)
                if r == 0:
                    tabs[kind] = jnp.where(hit, sa * BLOCKS + slot, tabs[kind])
                tabs[2 + 2 * r + kind] = jnp.where(hit, offset, tabs[2 + 2 * r + kind])
        return tuple(tabs)

    loads[0].wait()
    loads[1].wait()
    tabs = lax.fori_loop(0, GBX, fill, tuple(jnp.zeros((1, BW), jnp.int32) for _ in range(8)))
    for i in range(8):
        tab_v[pl.ds(i, 1), :] = tabs[i]
    load_tab = pltpu.make_async_copy(tab_v, tab_s, lsem.at[9])
    load_tab.start()

    mine = a * BLOCKS
    for load in loads[2:6]:
        load.wait()
    wet = wet_ref[...]
    total = jnp.zeros(wet.shape, jnp.float32)
    for k in range(LEV):
        total = total + jnp.where(wet > k, buoy_ref[k].astype(jnp.float32), 0.0)
    fields = (total, wet.astype(jnp.float32), prior_ref[...])
    for q in range(3):
        for n in range(BLOCKS):
            for r in range(BH):
                gat[mine + n, q, pl.ds(r, 1), :] = fields[q][n : n + 1, r * BW : (r + 1) * BW]
    for n in range(BLOCKS):
        gat[mine + n, 3] = land_ref[n].astype(jnp.float32)

    pl.semaphore_wait(barrier, greeted)

    def remote(src, dst, tag, where):
        copy = pltpu.make_async_remote_copy(
            src_ref=src, dst_ref=dst, send_sem=ssem.at[tag], recv_sem=rsem.at[tag],
            device_id=where, device_id_type=MESH,
        )
        copy.start()
        return copy

    chunk = gat.at[pl.ds(mine, BLOCKS)]
    first = [remote(chunk, chunk, i - 1, {"bx": dev(i, 0)}) for i in range(1, 4)]

    for load in loads[6:]:
        load.wait()

    def run_columns(part):
        per = width // 128
        for i in PARTS[part]:
            streams[i].wait()
        chunks = PARTS[part]

        def body(t, carry):
            columns(t, tr, speed_ref, diff_ref, wet_ref, patch_ref, coef)
            return carry

        lax.fori_loop(chunks.start * per, chunks.stop * per, body, 0)

    run_columns(0)
    load_tab.wait()
    for copy in first:
        copy.wait()

    lane8 = lax.broadcasted_iota(jnp.int32, (8, BW), 1)
    window_of = lane8 // 8

    def window(q, n, side):
        return (q % 2) * 8 + 2 * n + side

    def turned(v, shift):
        return pltpu.roll(v, shift % BW, 1) if shift % BW else v

    def pack(dst, role, i):
        its_row = (row, below_row, above_row)[role]
        base = its_row * GBX + dev(0, i) * BLOCKS
        place = {}
        for n in range(BLOCKS):
            g = lax.rem(tmap[base + n], GBX)
            for side, shift in ((0, 1), (1, GBX - 1), (2, 0)):
                at = lax.rem(g + shift, GBX)
                place[0, n, side] = tab_s[0, at]
                place[1, n, side] = tab_s[1, at]
        halves = ((0, 1), (1,), (0,))[role]
        names = range(3) if role == 0 else range(4)
        t = 0
        for n in range(BLOCKS):
            for q in names:
                for h in halves:
                    dst[t] = gat[place[q // 3, n, 2], q, pl.ds(8 * h, 8), :]
                    t += 1
        for pair in range(2):
            for h in halves:
                tile = jnp.zeros((8, BW), jnp.float32)
                for q in (2 * pair, 2 * pair + 1):
                    for n in range(BLOCKS):
                        for side in range(2):
                            w = window(q, n, side)
                            v = gat[place[q // 3, n, side], q, pl.ds(8 * h, 8), :]
                            v = turned(v, 8 * w + (8 if side else 0))
                            tile = jnp.where(window_of == w, v, tile)
                dst[t] = tile
                t += 1

    second = []
    for i in (2, 1, 3, 0):
        for d in range(2):
            buf = send_row.at[d, i]
            pack(buf, 1 + d, i)
            to = below_row if d == 0 else above_row
            second.append(
                remote(buf, recv_row.at[d, i], 6 + 4 * d + i, {"by": to, "bx": dev(0, i)})
            )
        if i:
            buf = send_own.at[i - 1]
            pack(buf, 0, i)
            second.append(remote(buf, recv_own.at[i], 2 + i, {"bx": dev(0, i)}))
        else:
            pack(recv_own.at[0], 0, 0)
    run_columns(1)
    for copy in second:
        copy.wait()

    has_north = (row > 0).astype(jnp.float32)
    has_south = (row < NBY - 1).astype(jnp.float32)
    acc = [None] * len(PAIRS)
    for n in range(BLOCKS):
        g = lax.rem(tmap[row * GBX + me * BLOCKS + n], GBX)
        around = [lax.rem(g + shift, GBX) for shift in (1, GBX - 1, 0)]
        came = {
            (src, kind, side): tab_s[2 + 2 * src + kind, around[side]]
            for src in range(3) for kind in range(2) for side in range(3)
        }

        def beside(buf, src, q, at):
            east = buf[came[src, q // 3, 0], at]
            west = buf[came[src, q // 3, 1], at]
            east = turned(east, BW - 8 * window(q, n, 0))
            west = turned(west, BW - 8 - 8 * window(q, n, 1))
            return jnp.where(lane8 < 8, east, jnp.where(lane8 >= BW - 8, west, 0.0))

        whole = []
        for q in range(4):
            kind = q // 3
            ends = []
            for d in range(2):
                buf = recv_row.at[d]
                middle = buf[came[1 + d, kind, 2], n * 4 + q]
                end = jnp.concatenate([middle, beside(buf, 1 + d, q, 16 + q // 2)], axis=1)
                if q == 3:
                    end = end * (has_north if d == 0 else has_south)
                ends.append(end)
            parts = [ends[0]]
            for h in range(2):
                if q < 3:
                    middle = recv_own[came[0, 0, 2], (n * 3 + q) * 2 + h]
                else:
                    middle = gat[mine + n, 3, pl.ds(8 * h, 8), :]
                side = beside(recv_own, 0, q, 24 + (q // 2) * 2 + h)
                parts.append(jnp.concatenate([middle, side], axis=1))
            parts.append(ends[1])
            whole.append(jnp.concatenate(parts, axis=0))
        force, depth, prior, ocean = whole
        rows = BH + 16

        def east(v):
            return pltpu.roll(v, LANES - 1, 1)

        def west(v):
            return pltpu.roll(v, 1, 1)

        def south_of(v):
            return pltpu.roll(v, rows - 1, 0)

        def north_of(v):
            return pltpu.roll(v, 1, 0)

        face_e = FACE * jnp.minimum(depth, east(depth)) * ocean * east(ocean)
        face_s = FACE * jnp.minimum(depth, south_of(depth)) * ocean * south_of(ocean)
        face_w, face_n = west(face_e), north_of(face_s)
        centre = SURFACE * ocean + (1.0 - ocean)
        diag = centre + face_e + face_w + face_s + face_n
        inv = 1.0 / diag
        centre, face_e, face_w = centre * inv, face_e * inv, face_w * inv
        face_s, face_n = face_s * inv, face_n * inv

        def scaled(v):
            out = centre * v + face_e * (v - east(v)) + face_w * (v - west(v))
            return out + face_s * (v - south_of(v)) + face_n * (v - north_of(v))

        def own(v):
            return v[8 : 8 + BH, :BW]

        guess = ocean * prior
        u = ocean * force * inv - scaled(guess)
        weight = own(diag)
        basis[n, ITERS] = own(guess)
        mine_of, weighted = [], []
        for k in range(ITERS + 1):
            mine_of.append(own(u))
            if k < ITERS:
                basis[n, k] = mine_of[k]
                weighted.append(weight * mine_of[k])
                image = scaled(u)
                u = image - SHIFTS[k] * u if SHIFTS[k] else image
        for e, (i, j) in enumerate(PAIRS):
            prod = weighted[i] * mine_of[j]
            prod = prod[:8] + prod[8:]
            acc[e] = prod if acc[e] is None else acc[e] + prod

    for e in range(len(PAIRS)):
        gram[pl.ds(e, 1), :] = jnp.sum(acc[e], axis=0, keepdims=True)
    gram[pl.ds(len(PAIRS), ENTRIES - len(PAIRS)), :] = jnp.zeros(
        (ENTRIES - len(PAIRS), BW), jnp.float32
    )
    on_diag = lax.broadcasted_iota(jnp.int32, (ENTRIES, BW), 0) == lax.broadcasted_iota(
        jnp.int32, (ENTRIES, BW), 1
    )
    placed = jnp.where(on_diag, jnp.sum(gram[...], axis=1, keepdims=True), 0.0)
    packed = placed[0:8] + placed[8:16] + placed[16:24] + placed[24:32]

    def all_sum(value, ring, index, count, axis, base, during):
        ring[index] = value
        sent = [
            remote(ring.at[index], ring.at[index], base + i, {axis: lax.rem(index + i, count)})
            for i in range(1, count)
        ]
        if during:
            run_columns(2)
        for copy in sent:
            copy.wait()
        return jnp.sum(ring[...], axis=0)

    packed = all_sum(packed, ring_a, me, NBX, "bx", 14, True)
    packed = all_sum(packed, ring_b, row, NBY, "by", 14 + NBX, False)
    line = jnp.sum(packed, axis=0, keepdims=True)
    spread = jnp.sum(jnp.where(on_diag, line, 0.0), axis=1, keepdims=True)
    spread = jnp.broadcast_to(spread, (ENTRIES, BW))
    g = {}
    for e, (i, j) in enumerate(PAIRS):
        g[i, j] = g[j, i] = spread[e : e + 1]

    def form(left, right):
        out = None
        for i, vi in enumerate(left):
            inner = None
            for j, vj in enumerate(right):
                term = g[i, j] * vj
                inner = term if inner is None else inner + term
            out = vi * inner if out is None else out + vi * inner
        return out

    one = jnp.ones((1, BW), jnp.float32)
    zero = jnp.zeros((1, BW), jnp.float32)
    p, z = [one], [one]
    x = [zero] * ITERS
    rz = g[0, 0]
    for it in range(ITERS):
        y = [SHIFTS[k] * p[k] if SHIFTS[k] else zero for k in range(it + 1)] + [zero]
        for k in range(it + 1):
            y[k + 1] = y[k + 1] + p[k]
        pq = form(p, y)
        live = jnp.logical_and(rz > 0.0, pq > 0.0)
        alpha = jnp.where(live, rz, 0.0) / jnp.where(live, pq, 1.0)
        alpha = jnp.minimum(alpha, ALPHA_MAX)
        for k in range(it + 1):
            x[k] = x[k] + alpha * p[k]
        if it + 1 < ITERS:
            z = [zk - alpha * yk for zk, yk in zip(z + [zero], y)]
            rz_new = jnp.maximum(form(z, z), 0.0)
            beta = jnp.where(live, rz_new, 0.0) / jnp.where(live, rz, 1.0)
            p = [zk + beta * pk for zk, pk in zip(z, p + [zero])]
            rz = rz_new
    for n in range(BLOCKS):
        height = basis[n, ITERS]
        for k in range(ITERS):
            height = height + x[k] * basis[n, k]
        out_ref[n] = height


def write_kernel(tr, height, tr_out, height_out, sem):
    width = CELLS // CHUNKS
    copies = [pltpu.make_async_copy(height, height_out, sem.at[CHUNKS])]
    for i in range(CHUNKS):
        part = (slice(None), slice(None), slice(None), pl.ds(i * width, width))
        copies.append(pltpu.make_async_copy(tr.at[part], tr_out.at[part], sem.at[i]))
    for copy in copies:
        copy.start()
    for copy in copies:
        copy.wait()


def local(
    tracers, vertical_speed, diffusivity, buoyancy_force, wet_levels, surface_patch,
    prior_height, land_mask, baroclinic_map, barotropic_map,
):
    f32, i32 = jnp.float32, jnp.int32
    vmem = pl.BlockSpec(memory_space=pltpu.VMEM)
    hbm = pl.BlockSpec(memory_space=pltpu.HBM)
    tags = 14 + NBX + NBY
    height_shape = (BLOCKS, BH, BW)
    tr, height = pl.pallas_call(
        step_kernel,
        out_shape=(pltpu.VMEM(tracers.shape, f32), pltpu.VMEM(height_shape, f32)),
        in_specs=[hbm] * 10,
        out_specs=(vmem, vmem),
        scratch_shapes=[
            pltpu.SMEM((NBY * GBX,), i32),
            pltpu.SMEM((NBY * GBX,), i32),
            pltpu.VMEM((LEV, BLOCKS, CELLS), jnp.bfloat16),
            pltpu.VMEM((BLOCKS, CELLS), i32),
            pltpu.VMEM((BLOCKS, CELLS), i32),
            pltpu.VMEM((BLOCKS, CELLS), f32),
            pltpu.VMEM(height_shape, i32),
            pltpu.VMEM((LEV, BLOCKS, CELLS), f32),
            pltpu.VMEM((LEV, BLOCKS, CELLS), f32),
            pltpu.VMEM((6, LEV, BLOCKS, 128), f32),
            pltpu.VMEM((4 * BLOCKS, 4, BH, BW), f32),
            pltpu.VMEM((3, OWN_TILES, 8, BW), f32),
            pltpu.VMEM((4, OWN_TILES, 8, BW), f32),
            pltpu.VMEM((2, 4, ROW_TILES, 8, BW), f32),
            pltpu.VMEM((2, 4, ROW_TILES, 8, BW), f32),
            pltpu.VMEM((BLOCKS, ITERS + 1, BH, BW), f32),
            pltpu.VMEM((ENTRIES, BW), f32),
            pltpu.VMEM((NBX, 8, BW), f32),
            pltpu.VMEM((NBY, 8, BW), f32),
            pltpu.VMEM((8, BW), i32),
            pltpu.SMEM((8, BW), i32),
            pltpu.SemaphoreType.DMA((10,)),
            pltpu.SemaphoreType.DMA((CHUNKS,)),
            pltpu.SemaphoreType.DMA((tags,)),
            pltpu.SemaphoreType.DMA((tags,)),
        ],
        compiler_params=pltpu.CompilerParams(
            collective_id=0, has_side_effects=True, vmem_limit_bytes=32 * 2**20
        ),
        name="step",
    )(
        *(
            pltpu.with_memory_space_constraint(array, pltpu.HBM)
            for array in (
                baroclinic_map, barotropic_map, buoyancy_force, wet_levels, surface_patch,
                prior_height, land_mask, vertical_speed, diffusivity, tracers,
            )
        )
    )
    return pl.pallas_call(
        write_kernel,
        out_shape=(
            jax.ShapeDtypeStruct(tracers.shape, f32), jax.ShapeDtypeStruct(height_shape, f32)
        ),
        in_specs=[vmem, vmem],
        out_specs=(hbm, hbm),
        scratch_shapes=[pltpu.SemaphoreType.DMA((CHUNKS + 1,))],
        compiler_params=pltpu.CompilerParams(vmem_limit_bytes=2 * 2**20),
        name="write",
    )(tr, height)


def solution(mesh):
    return jax.shard_map(
        local,
        mesh=mesh,
        in_specs=(
            P(None, ("by", "bx"), None, None),
            P(None, ("by", "bx"), None),
            P(None, ("by", "bx"), None),
            P(None, ("by", "bx"), None),
            P(("by", "bx"), None),
            P(("by", "bx"), None),
            P(("by", "bx"), None),
            P(("by", "bx"), None, None),
            P(),
            P(),
        ),
        out_specs=(P(None, ("by", "bx"), None, None), P(("by", "bx"), None, None)),
        check_vma=False,
    )
```

```python
import jax
import jax.numpy as jnp
from jax import lax
from jax.experimental import pallas as pl
from jax.experimental.pallas import tpu as pltpu
from jax.sharding import PartitionSpec as P

MESH = pl.DeviceIdType.MESH
ITERS = 6
RESTORE = 0.5
SURFACE = 0.1
FACE_SCALE = 2.0
LEV, TR, BH, BW = 20, 16, 16, 128
CELLS = BH * BW
GBX, BLOCKS, NBX, NBY = 64, 4, 16, 8
LANES = 256
FACE = FACE_SCALE / LEV
SHIFTS = (0.0, 2.0, 1.0, 1.577, 0.4226, 0.1)
ALPHA_MAX = 82.0
PAIRS = [(i, j) for i in range(ITERS) for j in range(i, ITERS + 1)]
ENTRIES = 32
CHUNKS = 8
PARTS = (range(0, 1), range(1, 5), range(5, 8))
OWN_PART = ((0, 18), (18, 10))
ROW_PART = ((0, 9), (9, 9))
DEVICES = NBX * NBY
SUM_TAG = 28


def columns(tile, tr, speed_ref, diff_ref, wet_ref, patch_ref, coef):
    sl = pl.ds(pl.multiple_of(tile * 128, 128), 128)
    wet = wet_ref[:, sl]
    zero = jnp.zeros(wet.shape, jnp.float32)
    mix_above, pos_above, neg_above, ratio_above = zero, zero, zero, zero
    for k in range(LEV):
        is_wet = (wet > k).astype(jnp.float32)
        is_open = (wet > k + 1).astype(jnp.float32)
        speed = speed_ref[k, :, sl] * is_open
        pos, neg = jnp.maximum(speed, 0.0), jnp.minimum(speed, 0.0)
        mix = diff_ref[k, :, sl] * is_open
        pivot = 1.0 + mix + mix_above
        if k == 0:
            pivot = pivot + RESTORE * is_wet
        pivot = pivot - mix_above * ratio_above
        inv = 1.0 / pivot
        scale = is_wet * inv
        coef[0, k] = scale * (1.0 + neg - pos_above)
        coef[1, k] = scale * pos
        coef[2, k] = -scale * neg_above
        coef[3, k] = mix_above * inv
        ratio = mix * inv
        coef[4, k] = ratio
        if k == 0:
            coef[5, 0] = RESTORE * scale
        mix_above, pos_above, neg_above, ratio_above = mix, pos, neg, ratio
    ids = lax.broadcasted_iota(jnp.int32, (TR, 128), 0)
    for n in range(BLOCKS):

        def c(i, k):
            return coef[i, k, pl.ds(n, 1), :]

        values = []
        above, here, value = None, tr[0, n, :, sl], None
        for k in range(LEV):
            new = c(0, k) * here
            if k + 1 < LEV:
                below = tr[k + 1, n, :, sl]
                new = new + c(1, k) * below
            if k == 0:
                target = patch_ref[pl.ds(n, 1), sl] == ids
                new = new + jnp.where(target, c(5, 0), 0.0)
            else:
                new = new + c(2, k) * above + c(3, k) * value
            value = new
            values.append(value)
            above, here = here, below
        follow = values[-1]
        tr[LEV - 1, n, :, sl] = follow
        for k in range(LEV - 2, -1, -1):
            follow = values[k] + c(4, k) * follow
            tr[k, n, :, sl] = follow


def step_kernel(
    cmap_hbm, tmap_hbm, buoy_hbm, wet_hbm, patch_hbm, prior_hbm, land_hbm, speed_hbm, diff_hbm, tr_hbm,
    tr, out_ref,
    cmap, tmap, buoy_ref, wet_ref, patch_ref, prior_ref, land_ref, speed_ref, diff_ref, coef,
    depths, forces, send_own, recv_own, send_row, recv_row, basis, gram, ring,
    tab_v, tab_s, plane_sem, all_sem, lsem, tsem, ssem, rsem,
):
    row = lax.axis_index("by")
    me = lax.axis_index("bx")
    core = lax.rem(row, 2)
    below_row = lax.rem(row + 1, NBY)
    above_row = lax.rem(row + NBY - 1, NBY)
    step_a = 4 - 3 * core
    step_b = 1 + 3 * core
    px, py = me // 4, lax.rem(me, 4)
    a = px + core * (py - px)
    b = py + core * (px - py)

    def dev(i, j):
        return lax.rem(a + i, 4) * step_a + lax.rem(b + j, 4) * step_b

    barrier = pltpu.get_barrier_semaphore()

    def greet(**where):
        pl.semaphore_signal(barrier, inc=1, device_id=where, device_id_type=MESH)

    for i in range(1, 4):
        greet(bx=dev(i, 0))
        greet(bx=dev(0, i))
        greet(by=below_row, bx=dev(0, i))
        greet(by=above_row, bx=dev(0, i))
        greet(by=below_row, bx=dev(i, 0))
        greet(by=above_row, bx=dev(i, 0))
    for i in range(1, NBY):
        greet(by=lax.rem(row + i, NBY))
    greeted = 6 * 3 + NBY - 1

    local = [
        (wet_hbm, wet_ref), (prior_hbm, prior_ref), (buoy_hbm, buoy_ref), (land_hbm, land_ref),
        (cmap_hbm, cmap), (tmap_hbm, tmap),
        (speed_hbm, speed_ref), (diff_hbm, diff_ref), (patch_hbm, patch_ref),
    ]
    loads = [pltpu.make_async_copy(s, d, lsem.at[i]) for i, (s, d) in enumerate(local)]
    for load in loads[:6]:
        load.start()

    def remote(src, dst, tag, where):
        copy = pltpu.make_async_remote_copy(
            src_ref=src, dst_ref=dst, send_sem=ssem.at[tag], recv_sem=rsem.at[tag],
            device_id=where, device_id_type=MESH,
        )
        copy.start()
        return copy

    mine = a * BLOCKS
    gat = (depths, forces)

    def place_field(pair, q, value):
        for n in range(BLOCKS):
            for r in range(BH):
                gat[pair][mine + n, q, pl.ds(r, 1), :] = value[n : n + 1, r * BW : (r + 1) * BW]

    def share(pair):
        chunk = gat[pair].at[pl.ds(mine, BLOCKS)]
        return [remote(chunk, chunk, 3 * pair + i - 1, {"bx": dev(i, 0)}) for i in range(1, 4)]

    loads[0].wait()
    loads[1].wait()
    wet = wet_ref[...]
    place_field(0, 0, wet.astype(jnp.float32))
    place_field(0, 1, prior_ref[...])
    pl.semaphore_wait(barrier, greeted)
    first = [share(0)]
    for i in range(1, 4):
        pl.semaphore_signal(plane_sem, inc=1, device_id={"bx": dev(0, i)}, device_id_type=MESH)

    loads[2].wait()
    loads[3].wait()
    total = jnp.zeros(wet.shape, jnp.float32)
    for k in range(LEV):
        total = total + jnp.where(wet > k, buoy_ref[k].astype(jnp.float32), 0.0)
    place_field(1, 0, total)
    for n in range(BLOCKS):
        gat[1][mine + n, 1] = land_ref[n].astype(jnp.float32)
    first.append(share(1))

    for load in loads[6:]:
        load.start()
    width = CELLS // CHUNKS
    streams = []
    for i in range(CHUNKS):
        part = (slice(None), slice(None), slice(None), pl.ds(i * width, width))
        streams.append(pltpu.make_async_copy(tr_hbm.at[part], tr.at[part], tsem.at[i]))
        streams[i].start()

    lane = lax.broadcasted_iota(jnp.int32, (1, BW), 1)
    sources = ((row, core, b), (above_row, 1 - core, a), (below_row, 1 - core, a))

    def fill(s, tabs):
        tabs = list(tabs)
        sx, sy, slot = s // 16, lax.rem(s // 4, 4), lax.rem(s, 4)
        for r, (which, its_core, its_b) in enumerate(sources):
            sa = sx + its_core * (sy - sx)
            sb = sy + its_core * (sx - sy)
            offset = lax.rem(its_b - sb + 4, 4)
            for kind, ref in enumerate((cmap, tmap)):
                hit = lane == lax.rem(ref[which * GBX + s], GBX)
                if r == 0:
                    tabs[kind] = jnp.where(hit, sa * BLOCKS + slot, tabs[kind])
                tabs[2 + 2 * r + kind] = jnp.where(hit, offset, tabs[2 + 2 * r + kind])
        return tuple(tabs)

    loads[4].wait()
    loads[5].wait()
    tabs = lax.fori_loop(0, GBX, fill, tuple(jnp.zeros((1, BW), jnp.int32) for _ in range(8)))
    for i in range(8):
        tab_v[pl.ds(i, 1), :] = tabs[i]
    load_tab = pltpu.make_async_copy(tab_v, tab_s, lsem.at[9])
    load_tab.start()

    pl.semaphore_wait(plane_sem, 3)
    for i in range(1, NBY):
        pl.semaphore_signal(
            all_sem, inc=1, device_id={"by": lax.rem(row + i, NBY)}, device_id_type=MESH
        )
    for load in loads[6:]:
        load.wait()

    def run_columns(part):
        per = width // 128
        for i in PARTS[part]:
            streams[i].wait()
        chunks = PARTS[part]

        def body(t, carry):
            columns(t, tr, speed_ref, diff_ref, wet_ref, patch_ref, coef)
            return carry

        lax.fori_loop(chunks.start * per, chunks.stop * per, body, 0)

    load_tab.wait()

    lane8 = lax.broadcasted_iota(jnp.int32, (8, BW), 1)
    window_of = lane8 // 8

    def window(q, n, side):
        return q * 8 + 2 * n + side

    def kind_of(pair, q):
        return 1 if (pair, q) == (1, 1) else 0

    def turned(v, shift):
        return pltpu.roll(v, shift % BW, 1) if shift % BW else v

    def pack(dst, pair, role, i):
        its_row = (row, below_row, above_row)[role]
        base = its_row * GBX + dev(0, i) * BLOCKS
        place = {}
        for n in range(BLOCKS):
            g = lax.rem(tmap[base + n], GBX)
            for side, shift in ((0, 1), (1, GBX - 1), (2, 0)):
                at = lax.rem(g + shift, GBX)
                for kind in range(1 + pair):
                    place[kind, n, side] = tab_s[kind, at]
        halves = ((0, 1), (1,), (0,))[role]
        t = (OWN_PART if role == 0 else ROW_PART)[pair][0]
        for n in range(BLOCKS):
            for q in range(1 if (role, pair) == (0, 1) else 2):
                for h in halves:
                    dst[t] = gat[pair][place[kind_of(pair, q), n, 2], q, pl.ds(8 * h, 8), :]
                    t += 1
        for h in halves:
            tile = jnp.zeros((8, BW), jnp.float32)
            for q in range(2):
                for n in range(BLOCKS):
                    for side in range(2):
                        w = window(q, n, side)
                        v = gat[pair][place[kind_of(pair, q), n, side], q, pl.ds(8 * h, 8), :]
                        v = turned(v, 8 * w + (8 if side else 0))
                        tile = jnp.where(window_of == w, v, tile)
            dst[t] = tile
            t += 1

    second = []
    for pair in range(2):
        for copy in first[pair]:
            copy.wait()
        row_part, own_part = pl.ds(*ROW_PART[pair]), pl.ds(*OWN_PART[pair])
        for i in (2, 1, 3, 0):
            for d in range(2):
                pack(send_row.at[d, i], pair, 1 + d, i)
                to = below_row if d == 0 else above_row
                second.append(
                    remote(
                        send_row.at[d, i, row_part], recv_row.at[d, i, row_part],
                        12 + 8 * pair + 4 * d + i, {"by": to, "bx": dev(0, i)},
                    )
                )
            if i:
                pack(send_own.at[i - 1], pair, 0, i)
                second.append(
                    remote(
                        send_own.at[i - 1, own_part], recv_own.at[i, own_part],
                        5 + 3 * pair + i, {"bx": dev(0, i)},
                    )
                )
            else:
                pack(recv_own.at[0], pair, 0, 0)
        if pair == 0:
            run_columns(0)
    run_columns(1)
    for copy in second:
        copy.wait()

    has_north = (row > 0).astype(jnp.float32)
    has_south = (row < NBY - 1).astype(jnp.float32)
    acc = [None] * len(PAIRS)
    for n in range(BLOCKS):
        g = lax.rem(tmap[row * GBX + me * BLOCKS + n], GBX)
        around = [lax.rem(g + shift, GBX) for shift in (1, GBX - 1, 0)]
        came = {
            (src, kind, side): tab_s[2 + 2 * src + kind, around[side]]
            for src in range(3) for kind in range(2) for side in range(3)
        }

        def beside(buf, src, pair, q, at):
            kind = kind_of(pair, q)
            east = turned(buf[came[src, kind, 0], at], BW - 8 * window(q, n, 0))
            west = turned(buf[came[src, kind, 1], at], BW - 8 - 8 * window(q, n, 1))
            return jnp.where(lane8 < 8, east, jnp.where(lane8 >= BW - 8, west, 0.0))

        whole = {}
        for pair in range(2):
            row_base, own_base = ROW_PART[pair][0], OWN_PART[pair][0]
            for q in range(2):
                kind = kind_of(pair, q)
                ends = []
                for d in range(2):
                    buf = recv_row.at[d]
                    middle = buf[came[1 + d, kind, 2], row_base + n * 2 + q]
                    side = beside(buf, 1 + d, pair, q, row_base + 8)
                    end = jnp.concatenate([middle, side], axis=1)
                    if kind:
                        end = end * (has_north if d == 0 else has_south)
                    ends.append(end)
                parts = [ends[0]]
                for h in range(2):
                    if kind:
                        middle = gat[1][mine + n, 1, pl.ds(8 * h, 8), :]
                    elif pair:
                        middle = recv_own[came[0, 0, 2], own_base + n * 2 + h]
                    else:
                        middle = recv_own[came[0, 0, 2], own_base + (n * 2 + q) * 2 + h]
                    edges = own_base + (8 if pair else 16)
                    side = beside(recv_own, 0, pair, q, edges + h)
                    parts.append(jnp.concatenate([middle, side], axis=1))
                parts.append(ends[1])
                whole[pair, q] = jnp.concatenate(parts, axis=0)
        depth, prior, force, ocean = whole[0, 0], whole[0, 1], whole[1, 0], whole[1, 1]
        rows = BH + 16

        def east(v):
            return pltpu.roll(v, LANES - 1, 1)

        def west(v):
            return pltpu.roll(v, 1, 1)

        def south_of(v):
            return pltpu.roll(v, rows - 1, 0)

        def north_of(v):
            return pltpu.roll(v, 1, 0)

        face_e = FACE * jnp.minimum(depth, east(depth)) * ocean * east(ocean)
        face_s = FACE * jnp.minimum(depth, south_of(depth)) * ocean * south_of(ocean)
        face_w, face_n = west(face_e), north_of(face_s)
        centre = SURFACE * ocean + (1.0 - ocean)
        diag = centre + face_e + face_w + face_s + face_n
        inv = 1.0 / diag
        centre, face_e, face_w = centre * inv, face_e * inv, face_w * inv
        face_s, face_n = face_s * inv, face_n * inv

        def scaled(v):
            out = centre * v + face_e * (v - east(v)) + face_w * (v - west(v))
            return out + face_s * (v - south_of(v)) + face_n * (v - north_of(v))

        def own(v):
            return v[8 : 8 + BH, :BW]

        guess = ocean * prior
        u = ocean * force * inv - scaled(guess)
        weight = own(diag)
        basis[n, ITERS] = own(guess)
        mine_of, weighted = [], []
        for k in range(ITERS + 1):
            mine_of.append(own(u))
            if k < ITERS:
                basis[n, k] = mine_of[k]
                weighted.append(weight * mine_of[k])
                image = scaled(u)
                u = image - SHIFTS[k] * u if SHIFTS[k] else image
        for e, (i, j) in enumerate(PAIRS):
            prod = weighted[i] * mine_of[j]
            prod = prod[:8] + prod[8:]
            acc[e] = prod if acc[e] is None else acc[e] + prod

    for e in range(len(PAIRS)):
        gram[pl.ds(e, 1), :] = jnp.sum(acc[e], axis=0, keepdims=True)
    gram[pl.ds(len(PAIRS), ENTRIES - len(PAIRS)), :] = jnp.zeros(
        (ENTRIES - len(PAIRS), BW), jnp.float32
    )
    on_diag = lax.broadcasted_iota(jnp.int32, (ENTRIES, BW), 0) == lax.broadcasted_iota(
        jnp.int32, (ENTRIES, BW), 1
    )
    placed = jnp.where(on_diag, jnp.sum(gram[...], axis=1, keepdims=True), 0.0)
    packed = placed[0:8] + placed[8:16] + placed[16:24] + placed[24:32]

    pl.semaphore_wait(all_sem, NBY - 1)
    flat = row * NBX + me
    ring[flat] = jnp.sum(packed, axis=0, keepdims=True)
    for i in range(1, DEVICES):
        to = lax.rem(flat + i, DEVICES)
        remote(ring.at[flat], ring.at[flat], SUM_TAG, {"by": to // NBX, "bx": lax.rem(to, NBX)})
    run_columns(2)
    others = ring.at[pl.ds(0, DEVICES - 1)]
    pltpu.make_async_copy(others, others, rsem.at[SUM_TAG]).wait()
    pltpu.make_async_copy(others, others, ssem.at[SUM_TAG]).wait()
    line = jnp.sum(ring[...], axis=0)
    spread = jnp.sum(jnp.where(on_diag, line, 0.0), axis=1, keepdims=True)
    spread = jnp.broadcast_to(spread, (ENTRIES, BW))
    g = {}
    for e, (i, j) in enumerate(PAIRS):
        g[i, j] = g[j, i] = spread[e : e + 1]

    def form(left, right):
        out = None
        for i, vi in enumerate(left):
            inner = None
            for j, vj in enumerate(right):
                term = g[i, j] * vj
                inner = term if inner is None else inner + term
            out = vi * inner if out is None else out + vi * inner
        return out

    one = jnp.ones((1, BW), jnp.float32)
    zero = jnp.zeros((1, BW), jnp.float32)
    p, z = [one], [one]
    x = [zero] * ITERS
    rz = g[0, 0]
    for it in range(ITERS):
        y = [SHIFTS[k] * p[k] if SHIFTS[k] else zero for k in range(it + 1)] + [zero]
        for k in range(it + 1):
            y[k + 1] = y[k + 1] + p[k]
        pq = form(p, y)
        live = jnp.logical_and(rz > 0.0, pq > 0.0)
        alpha = jnp.where(live, rz, 0.0) / jnp.where(live, pq, 1.0)
        alpha = jnp.minimum(alpha, ALPHA_MAX)
        for k in range(it + 1):
            x[k] = x[k] + alpha * p[k]
        if it + 1 < ITERS:
            z = [zk - alpha * yk for zk, yk in zip(z + [zero], y)]
            rz_new = jnp.maximum(form(z, z), 0.0)
            beta = jnp.where(live, rz_new, 0.0) / jnp.where(live, rz, 1.0)
            p = [zk + beta * pk for zk, pk in zip(z, p + [zero])]
            rz = rz_new
    for n in range(BLOCKS):
        height = basis[n, ITERS]
        for k in range(ITERS):
            height = height + x[k] * basis[n, k]
        out_ref[n] = height


def write_kernel(tr, height, tr_out, height_out, sem):
    width = CELLS // CHUNKS
    copies = [pltpu.make_async_copy(height, height_out, sem.at[CHUNKS])]
    for i in range(CHUNKS):
        part = (slice(None), slice(None), slice(None), pl.ds(i * width, width))
        copies.append(pltpu.make_async_copy(tr.at[part], tr_out.at[part], sem.at[i]))
    for copy in copies:
        copy.start()
    for copy in copies:
        copy.wait()


def local(
    tracers, vertical_speed, diffusivity, buoyancy_force, wet_levels, surface_patch,
    prior_height, land_mask, baroclinic_map, barotropic_map,
):
    f32, i32 = jnp.float32, jnp.int32
    vmem = pl.BlockSpec(memory_space=pltpu.VMEM)
    hbm = pl.BlockSpec(memory_space=pltpu.HBM)
    tags = SUM_TAG + 1
    height_shape = (BLOCKS, BH, BW)
    tr, height = pl.pallas_call(
        step_kernel,
        out_shape=(pltpu.VMEM(tracers.shape, f32), pltpu.VMEM(height_shape, f32)),
        in_specs=[hbm] * 10,
        out_specs=(vmem, vmem),
        scratch_shapes=[
            pltpu.SMEM((NBY * GBX,), i32),
            pltpu.SMEM((NBY * GBX,), i32),
            pltpu.VMEM((LEV, BLOCKS, CELLS), jnp.bfloat16),
            pltpu.VMEM((BLOCKS, CELLS), i32),
            pltpu.VMEM((BLOCKS, CELLS), i32),
            pltpu.VMEM((BLOCKS, CELLS), f32),
            pltpu.VMEM(height_shape, i32),
            pltpu.VMEM((LEV, BLOCKS, CELLS), f32),
            pltpu.VMEM((LEV, BLOCKS, CELLS), f32),
            pltpu.VMEM((6, LEV, BLOCKS, 128), f32),
            pltpu.VMEM((4 * BLOCKS, 2, BH, BW), f32),
            pltpu.VMEM((4 * BLOCKS, 2, BH, BW), f32),
            pltpu.VMEM((3, 28, 8, BW), f32),
            pltpu.VMEM((4, 28, 8, BW), f32),
            pltpu.VMEM((2, 4, 18, 8, BW), f32),
            pltpu.VMEM((2, 4, 18, 8, BW), f32),
            pltpu.VMEM((BLOCKS, ITERS + 1, BH, BW), f32),
            pltpu.VMEM((ENTRIES, BW), f32),
            pltpu.VMEM((DEVICES, 1, BW), f32),
            pltpu.VMEM((8, BW), i32),
            pltpu.SMEM((8, BW), i32),
            pltpu.SemaphoreType.REGULAR,
            pltpu.SemaphoreType.REGULAR,
            pltpu.SemaphoreType.DMA((10,)),
            pltpu.SemaphoreType.DMA((CHUNKS,)),
            pltpu.SemaphoreType.DMA((tags,)),
            pltpu.SemaphoreType.DMA((tags,)),
        ],
        compiler_params=pltpu.CompilerParams(
            collective_id=0, has_side_effects=True, vmem_limit_bytes=32 * 2**20
        ),
        name="step",
    )(
        *(
            pltpu.with_memory_space_constraint(array, pltpu.HBM)
            for array in (
                baroclinic_map, barotropic_map, buoyancy_force, wet_levels, surface_patch,
                prior_height, land_mask, vertical_speed, diffusivity, tracers,
            )
        )
    )
    return pl.pallas_call(
        write_kernel,
        out_shape=(
            jax.ShapeDtypeStruct(tracers.shape, f32), jax.ShapeDtypeStruct(height_shape, f32)
        ),
        in_specs=[vmem, vmem],
        out_specs=(hbm, hbm),
        scratch_shapes=[pltpu.SemaphoreType.DMA((CHUNKS + 1,))],
        compiler_params=pltpu.CompilerParams(vmem_limit_bytes=2 * 2**20),
        name="write",
    )(tr, height)


def solution(mesh):
    return jax.shard_map(
        local,
        mesh=mesh,
        in_specs=(
            P(None, ("by", "bx"), None, None),
            P(None, ("by", "bx"), None),
            P(None, ("by", "bx"), None),
            P(None, ("by", "bx"), None),
            P(("by", "bx"), None),
            P(("by", "bx"), None),
            P(("by", "bx"), None),
            P(("by", "bx"), None, None),
            P(),
            P(),
        ),
        out_specs=(P(None, ("by", "bx"), None, None), P(("by", "bx"), None, None)),
        check_vma=False,
    )
```

```python
import jax
import jax.numpy as jnp
from jax import lax
from jax.experimental import pallas as pl
from jax.experimental.pallas import tpu as pltpu
from jax.sharding import PartitionSpec as P

MESH = pl.DeviceIdType.MESH
ITERS = 6
RESTORE = 0.5
SURFACE = 0.1
FACE_SCALE = 2.0
LEV, TR, BH, BW = 20, 16, 16, 128
CELLS = BH * BW
GBX, BLOCKS, NBX, NBY = 64, 4, 16, 8
LANES = 256
FACE = FACE_SCALE / LEV
SHIFTS = (0.0, 2.0, 1.0, 1.577, 0.4226, 0.1)
ALPHA_MAX = 82.0
PAIRS = [(i, j) for i in range(ITERS) for j in range(i, ITERS + 1)]
ENTRIES = 32
CHUNKS = 8
PARTS = (range(0, 1), range(1, 5), range(5, 8))
OWN_PART = ((0, 18), (18, 10))
ROW_PART = ((0, 9), (9, 9))
DEVICES = NBX * NBY
SUM_TAG = 28
FAR_FIRST = sorted(
    [(z, c, x, y) for z in range(4) for c in range(2) for x in range(4) for y in range(4)][1:],
    key=lambda o: -sum(min(k, 4 - k) for k in (o[0], o[2], o[3])),
)


def columns(tile, tr, speed_ref, diff_ref, wet_ref, patch_ref, coef):
    sl = pl.ds(pl.multiple_of(tile * 128, 128), 128)
    wet = wet_ref[:, sl]
    zero = jnp.zeros(wet.shape, jnp.float32)
    mix_above, pos_above, neg_above, ratio_above = zero, zero, zero, zero
    for k in range(LEV):
        is_wet = (wet > k).astype(jnp.float32)
        is_open = (wet > k + 1).astype(jnp.float32)
        speed = speed_ref[k, :, sl] * is_open
        pos, neg = jnp.maximum(speed, 0.0), jnp.minimum(speed, 0.0)
        mix = diff_ref[k, :, sl] * is_open
        pivot = 1.0 + mix + mix_above
        if k == 0:
            pivot = pivot + RESTORE * is_wet
        pivot = pivot - mix_above * ratio_above
        inv = 1.0 / pivot
        scale = is_wet * inv
        coef[0, k] = scale * (1.0 + neg - pos_above)
        coef[1, k] = scale * pos
        coef[2, k] = -scale * neg_above
        coef[3, k] = mix_above * inv
        ratio = mix * inv
        coef[4, k] = ratio
        if k == 0:
            coef[5, 0] = RESTORE * scale
        mix_above, pos_above, neg_above, ratio_above = mix, pos, neg, ratio
    ids = lax.broadcasted_iota(jnp.int32, (TR, 128), 0)
    for n in range(BLOCKS):

        def c(i, k):
            return coef[i, k, pl.ds(n, 1), :]

        values = []
        above, here, value = None, tr[0, n, :, sl], None
        for k in range(LEV):
            new = c(0, k) * here
            if k + 1 < LEV:
                below = tr[k + 1, n, :, sl]
                new = new + c(1, k) * below
            if k == 0:
                target = patch_ref[pl.ds(n, 1), sl] == ids
                new = new + jnp.where(target, c(5, 0), 0.0)
            else:
                new = new + c(2, k) * above + c(3, k) * value
            value = new
            values.append(value)
            above, here = here, below
        follow = values[-1]
        tr[LEV - 1, n, :, sl] = follow
        for k in range(LEV - 2, -1, -1):
            follow = values[k] + c(4, k) * follow
            tr[k, n, :, sl] = follow


def step_kernel(
    cmap_hbm, tmap_hbm, buoy_hbm, wet_hbm, patch_hbm, prior_hbm, land_hbm, speed_hbm, diff_hbm, tr_hbm,
    tr, out_ref,
    cmap, tmap, buoy_ref, wet_ref, patch_ref, prior_ref, land_ref, speed_ref, diff_ref, coef,
    depths, forces, send_own, recv_own, send_row, recv_row, basis, gram, ring,
    tab_v, tab_s, halo_sem, plane_sem, all_sem, lsem, tsem, ssem, rsem,
):
    row = lax.axis_index("by")
    me = lax.axis_index("bx")
    core = lax.rem(row, 2)
    below_row = lax.rem(row + 1, NBY)
    above_row = lax.rem(row + NBY - 1, NBY)
    step_a = 4 - 3 * core
    step_b = 1 + 3 * core
    px, py = me // 4, lax.rem(me, 4)
    a = px + core * (py - px)
    b = py + core * (px - py)

    def dev(i, j):
        return lax.rem(a + i, 4) * step_a + lax.rem(b + j, 4) * step_b

    barrier = pltpu.get_barrier_semaphore()

    def greet(**where):
        pl.semaphore_signal(barrier, inc=1, device_id=where, device_id_type=MESH)

    for i in range(1, 4):
        greet(bx=dev(i, 0))
        greet(bx=dev(0, i))
    for i in range(1, NBY):
        greet(by=lax.rem(row + i, NBY))
    greeted = 2 * 3 + NBY - 1

    local = [
        (wet_hbm, wet_ref), (prior_hbm, prior_ref), (buoy_hbm, buoy_ref), (land_hbm, land_ref),
        (cmap_hbm, cmap), (tmap_hbm, tmap),
        (speed_hbm, speed_ref), (diff_hbm, diff_ref), (patch_hbm, patch_ref),
    ]
    loads = [pltpu.make_async_copy(s, d, lsem.at[i]) for i, (s, d) in enumerate(local)]
    for load in loads[:6]:
        load.start()

    def remote(src, dst, tag, where):
        copy = pltpu.make_async_remote_copy(
            src_ref=src, dst_ref=dst, send_sem=ssem.at[tag], recv_sem=rsem.at[tag],
            device_id=where, device_id_type=MESH,
        )
        copy.start()
        return copy

    mine = a * BLOCKS
    gat = (depths, forces)

    def place_field(pair, q, value):
        for n in range(BLOCKS):
            for r in range(BH):
                gat[pair][mine + n, q, pl.ds(r, 1), :] = value[n : n + 1, r * BW : (r + 1) * BW]

    def share(pair):
        chunk = gat[pair].at[pl.ds(mine, BLOCKS)]
        return [remote(chunk, chunk, 3 * pair + i - 1, {"bx": dev(i, 0)}) for i in (2, 1, 3)]

    loads[0].wait()
    loads[1].wait()
    wet = wet_ref[...]
    place_field(0, 0, wet.astype(jnp.float32))
    place_field(0, 1, prior_ref[...])
    pl.semaphore_wait(barrier, greeted)
    first = [share(0)]
    for to in (below_row, above_row):
        pl.semaphore_signal(halo_sem, inc=1, device_id={"by": to}, device_id_type=MESH)
    for i in range(1, 4):
        pl.semaphore_signal(plane_sem, inc=1, device_id={"bx": dev(0, i)}, device_id_type=MESH)

    loads[2].wait()
    loads[3].wait()
    total = jnp.zeros(wet.shape, jnp.float32)
    for k in range(LEV):
        total = total + jnp.where(wet > k, buoy_ref[k].astype(jnp.float32), 0.0)
    place_field(1, 0, total)
    for n in range(BLOCKS):
        gat[1][mine + n, 1] = land_ref[n].astype(jnp.float32)
    first.append(share(1))

    for load in loads[6:]:
        load.start()
    width = CELLS // CHUNKS
    streams = []
    for i in range(CHUNKS):
        part = (slice(None), slice(None), slice(None), pl.ds(i * width, width))
        streams.append(pltpu.make_async_copy(tr_hbm.at[part], tr.at[part], tsem.at[i]))
        streams[i].start()

    lane = lax.broadcasted_iota(jnp.int32, (1, BW), 1)
    sources = ((row, core, b), (above_row, 1 - core, a), (below_row, 1 - core, a))

    def fill(s, tabs):
        tabs = list(tabs)
        sx, sy, slot = s // 16, lax.rem(s // 4, 4), lax.rem(s, 4)
        for r, (which, its_core, its_b) in enumerate(sources):
            sa = sx + its_core * (sy - sx)
            sb = sy + its_core * (sx - sy)
            offset = lax.rem(its_b - sb + 4, 4)
            for kind, ref in enumerate((cmap, tmap)):
                hit = lane == lax.rem(ref[which * GBX + s], GBX)
                if r == 0:
                    tabs[kind] = jnp.where(hit, sa * BLOCKS + slot, tabs[kind])
                tabs[2 + 2 * r + kind] = jnp.where(hit, offset, tabs[2 + 2 * r + kind])
        return tuple(tabs)

    loads[4].wait()
    loads[5].wait()
    tabs = lax.fori_loop(0, GBX, fill, tuple(jnp.zeros((1, BW), jnp.int32) for _ in range(8)))
    for i in range(8):
        tab_v[pl.ds(i, 1), :] = tabs[i]
    load_tab = pltpu.make_async_copy(tab_v, tab_s, lsem.at[9])
    load_tab.start()

    pl.semaphore_wait(plane_sem, 3)
    for i in range(1, NBY):
        pl.semaphore_signal(
            all_sem, inc=1, device_id={"by": lax.rem(row + i, NBY)}, device_id_type=MESH
        )
    def run_columns(part):
        if part == 0:
            for load in loads[6:]:
                load.wait()
        per = width // 128
        for i in PARTS[part]:
            streams[i].wait()
        chunks = PARTS[part]

        def body(t, carry):
            columns(t, tr, speed_ref, diff_ref, wet_ref, patch_ref, coef)
            return carry

        lax.fori_loop(chunks.start * per, chunks.stop * per, body, 0)

    load_tab.wait()

    lane8 = lax.broadcasted_iota(jnp.int32, (8, BW), 1)
    window_of = lane8 // 8

    def window(q, n, side):
        return q * 8 + 2 * n + side

    def kind_of(pair, q):
        return 1 if (pair, q) == (1, 1) else 0

    def turned(v, shift):
        return pltpu.roll(v, shift % BW, 1) if shift % BW else v

    def pack(dst, pair, role, i):
        its_row = (row, below_row, above_row)[role]
        base = its_row * GBX + dev(0, i) * BLOCKS
        place = {}
        for n in range(BLOCKS):
            g = lax.rem(tmap[base + n], GBX)
            for side, shift in ((0, 1), (1, GBX - 1), (2, 0)):
                at = lax.rem(g + shift, GBX)
                for kind in range(1 + pair):
                    place[kind, n, side] = tab_s[kind, at]
        halves = ((0, 1), (1,), (0,))[role]
        t = (OWN_PART if role == 0 else ROW_PART)[pair][0]
        for n in range(BLOCKS):
            for q in range(1 if (role, pair) == (0, 1) else 2):
                for h in halves:
                    dst[t] = gat[pair][place[kind_of(pair, q), n, 2], q, pl.ds(8 * h, 8), :]
                    t += 1
        for h in halves:
            tile = jnp.zeros((8, BW), jnp.float32)
            for q in range(2):
                for n in range(BLOCKS):
                    for side in range(2):
                        w = window(q, n, side)
                        v = gat[pair][place[kind_of(pair, q), n, side], q, pl.ds(8 * h, 8), :]
                        v = turned(v, 8 * w + (8 if side else 0))
                        tile = jnp.where(window_of == w, v, tile)
            dst[t] = tile
            t += 1

    pl.semaphore_wait(halo_sem, 2)
    second = []
    for pair in range(2):
        for copy in first[pair]:
            copy.wait_recv()
        row_part, own_part = pl.ds(*ROW_PART[pair]), pl.ds(*OWN_PART[pair])
        for i in (2, 1, 3, 0):
            for d in range(2):
                pack(send_row.at[d, i], pair, 1 + d, i)
                to = below_row if d == 0 else above_row
                second.append(
                    remote(
                        send_row.at[d, i, row_part], recv_row.at[d, i, row_part],
                        12 + 8 * pair + 4 * d + i, {"by": to, "bx": dev(0, i)},
                    )
                )
            if i:
                pack(send_own.at[i - 1], pair, 0, i)
                second.append(
                    remote(
                        send_own.at[i - 1, own_part], recv_own.at[i, own_part],
                        5 + 3 * pair + i, {"bx": dev(0, i)},
                    )
                )
            else:
                pack(recv_own.at[0], pair, 0, 0)
        if pair == 0:
            run_columns(0)
    run_columns(1)
    for copy in second:
        copy.wait_recv()

    has_north = (row > 0).astype(jnp.float32)
    has_south = (row < NBY - 1).astype(jnp.float32)
    acc = [None] * len(PAIRS)
    for n in range(BLOCKS):
        g = lax.rem(tmap[row * GBX + me * BLOCKS + n], GBX)
        around = [lax.rem(g + shift, GBX) for shift in (1, GBX - 1, 0)]
        came = {
            (src, kind, side): tab_s[2 + 2 * src + kind, around[side]]
            for src in range(3) for kind in range(2) for side in range(3)
        }

        def beside(buf, src, pair, q, at):
            kind = kind_of(pair, q)
            east = turned(buf[came[src, kind, 0], at], BW - 8 * window(q, n, 0))
            west = turned(buf[came[src, kind, 1], at], BW - 8 - 8 * window(q, n, 1))
            return jnp.where(lane8 < 8, east, jnp.where(lane8 >= BW - 8, west, 0.0))

        whole = {}
        for pair in range(2):
            row_base, own_base = ROW_PART[pair][0], OWN_PART[pair][0]
            for q in range(2):
                kind = kind_of(pair, q)
                ends = []
                for d in range(2):
                    buf = recv_row.at[d]
                    middle = buf[came[1 + d, kind, 2], row_base + n * 2 + q]
                    side = beside(buf, 1 + d, pair, q, row_base + 8)
                    end = jnp.concatenate([middle, side], axis=1)
                    if kind:
                        end = end * (has_north if d == 0 else has_south)
                    ends.append(end)
                parts = [ends[0]]
                for h in range(2):
                    if kind:
                        middle = gat[1][mine + n, 1, pl.ds(8 * h, 8), :]
                    elif pair:
                        middle = recv_own[came[0, 0, 2], own_base + n * 2 + h]
                    else:
                        middle = recv_own[came[0, 0, 2], own_base + (n * 2 + q) * 2 + h]
                    edges = own_base + (8 if pair else 16)
                    side = beside(recv_own, 0, pair, q, edges + h)
                    parts.append(jnp.concatenate([middle, side], axis=1))
                parts.append(ends[1])
                whole[pair, q] = jnp.concatenate(parts, axis=0)
        depth, prior, force, ocean = whole[0, 0], whole[0, 1], whole[1, 0], whole[1, 1]
        rows = BH + 16

        def east(v):
            return pltpu.roll(v, LANES - 1, 1)

        def west(v):
            return pltpu.roll(v, 1, 1)

        def south_of(v):
            return pltpu.roll(v, rows - 1, 0)

        def north_of(v):
            return pltpu.roll(v, 1, 0)

        face_e = FACE * jnp.minimum(depth, east(depth)) * ocean * east(ocean)
        face_s = FACE * jnp.minimum(depth, south_of(depth)) * ocean * south_of(ocean)
        face_w, face_n = west(face_e), north_of(face_s)
        centre = SURFACE * ocean + (1.0 - ocean)
        diag = centre + face_e + face_w + face_s + face_n
        inv = 1.0 / diag
        centre, face_e, face_w = centre * inv, face_e * inv, face_w * inv
        face_s, face_n = face_s * inv, face_n * inv

        def scaled(v):
            out = centre * v + face_e * (v - east(v)) + face_w * (v - west(v))
            return out + face_s * (v - south_of(v)) + face_n * (v - north_of(v))

        def own(v):
            return v[8 : 8 + BH, :BW]

        guess = ocean * prior
        u = ocean * force * inv - scaled(guess)
        weight = own(diag)
        basis[n, ITERS] = own(guess)
        mine_of, weighted = [], []
        for k in range(ITERS + 1):
            mine_of.append(own(u))
            if k < ITERS:
                basis[n, k] = mine_of[k]
                weighted.append(weight * mine_of[k])
                image = scaled(u)
                u = image - SHIFTS[k] * u if SHIFTS[k] else image
        for e, (i, j) in enumerate(PAIRS):
            prod = weighted[i] * mine_of[j]
            prod = prod[:8] + prod[8:]
            acc[e] = prod if acc[e] is None else acc[e] + prod

    for e in range(len(PAIRS)):
        gram[pl.ds(e, 1), :] = jnp.sum(acc[e], axis=0, keepdims=True)
    gram[pl.ds(len(PAIRS), ENTRIES - len(PAIRS)), :] = jnp.zeros(
        (ENTRIES - len(PAIRS), BW), jnp.float32
    )
    on_diag = lax.broadcasted_iota(jnp.int32, (ENTRIES, BW), 0) == lax.broadcasted_iota(
        jnp.int32, (ENTRIES, BW), 1
    )
    placed = jnp.where(on_diag, jnp.sum(gram[...], axis=1, keepdims=True), 0.0)
    packed = placed[0:8] + placed[8:16] + placed[16:24] + placed[24:32]

    pl.semaphore_wait(all_sem, NBY - 1)
    flat = row * NBX + me
    ring[flat] = jnp.sum(packed, axis=0, keepdims=True)
    for dz, dc, dx, dy in FAR_FIRST:
        to_row = lax.rem(row // 2 + dz, 4) * 2 + lax.rem(core + dc, 2)
        to = lax.rem(px + dx, 4) * 4 + lax.rem(py + dy, 4)
        remote(ring.at[flat], ring.at[flat], SUM_TAG, {"by": to_row, "bx": to})
    run_columns(2)
    others = ring.at[pl.ds(0, DEVICES - 1)]
    pltpu.make_async_copy(others, others, rsem.at[SUM_TAG]).wait()
    line = jnp.sum(ring[...], axis=0)
    spread = jnp.sum(jnp.where(on_diag, line, 0.0), axis=1, keepdims=True)
    spread = jnp.broadcast_to(spread, (ENTRIES, BW))
    g = {}
    for e, (i, j) in enumerate(PAIRS):
        g[i, j] = g[j, i] = spread[e : e + 1]

    def form(left, right):
        out = None
        for i, vi in enumerate(left):
            inner = None
            for j, vj in enumerate(right):
                term = g[i, j] * vj
                inner = term if inner is None else inner + term
            out = vi * inner if out is None else out + vi * inner
        return out

    one = jnp.ones((1, BW), jnp.float32)
    zero = jnp.zeros((1, BW), jnp.float32)
    p, z = [one], [one]
    x = [zero] * ITERS
    rz = g[0, 0]
    for it in range(ITERS):
        y = [SHIFTS[k] * p[k] if SHIFTS[k] else zero for k in range(it + 1)] + [zero]
        for k in range(it + 1):
            y[k + 1] = y[k + 1] + p[k]
        pq = form(p, y)
        live = jnp.logical_and(rz > 0.0, pq > 0.0)
        alpha = jnp.where(live, rz, 0.0) / jnp.where(live, pq, 1.0)
        alpha = jnp.minimum(alpha, ALPHA_MAX)
        for k in range(it + 1):
            x[k] = x[k] + alpha * p[k]
        if it + 1 < ITERS:
            z = [zk - alpha * yk for zk, yk in zip(z + [zero], y)]
            rz_new = jnp.maximum(form(z, z), 0.0)
            beta = jnp.where(live, rz_new, 0.0) / jnp.where(live, rz, 1.0)
            p = [zk + beta * pk for zk, pk in zip(z, p + [zero])]
            rz = rz_new
    pltpu.make_async_copy(others, others, ssem.at[SUM_TAG]).wait()
    for copy in first[0] + first[1] + second:
        copy.wait_send()
    for n in range(BLOCKS):
        height = basis[n, ITERS]
        for k in range(ITERS):
            height = height + x[k] * basis[n, k]
        out_ref[n] = height


def write_kernel(tr, height, tr_out, height_out, sem):
    width = CELLS // CHUNKS
    copies = [pltpu.make_async_copy(height, height_out, sem.at[CHUNKS])]
    for i in range(CHUNKS):
        part = (slice(None), slice(None), slice(None), pl.ds(i * width, width))
        copies.append(pltpu.make_async_copy(tr.at[part], tr_out.at[part], sem.at[i]))
    for copy in copies:
        copy.start()
    for copy in copies:
        copy.wait()


def local(
    tracers, vertical_speed, diffusivity, buoyancy_force, wet_levels, surface_patch,
    prior_height, land_mask, baroclinic_map, barotropic_map,
):
    f32, i32 = jnp.float32, jnp.int32
    vmem = pl.BlockSpec(memory_space=pltpu.VMEM)
    hbm = pl.BlockSpec(memory_space=pltpu.HBM)
    tags = SUM_TAG + 1
    height_shape = (BLOCKS, BH, BW)
    tr, height = pl.pallas_call(
        step_kernel,
        out_shape=(pltpu.VMEM(tracers.shape, f32), pltpu.VMEM(height_shape, f32)),
        in_specs=[hbm] * 10,
        out_specs=(vmem, vmem),
        scratch_shapes=[
            pltpu.SMEM((NBY * GBX,), i32),
            pltpu.SMEM((NBY * GBX,), i32),
            pltpu.VMEM((LEV, BLOCKS, CELLS), jnp.bfloat16),
            pltpu.VMEM((BLOCKS, CELLS), i32),
            pltpu.VMEM((BLOCKS, CELLS), i32),
            pltpu.VMEM((BLOCKS, CELLS), f32),
            pltpu.VMEM(height_shape, i32),
            pltpu.VMEM((LEV, BLOCKS, CELLS), f32),
            pltpu.VMEM((LEV, BLOCKS, CELLS), f32),
            pltpu.VMEM((6, LEV, BLOCKS, 128), f32),
            pltpu.VMEM((4 * BLOCKS, 2, BH, BW), f32),
            pltpu.VMEM((4 * BLOCKS, 2, BH, BW), f32),
            pltpu.VMEM((3, 28, 8, BW), f32),
            pltpu.VMEM((4, 28, 8, BW), f32),
            pltpu.VMEM((2, 4, 18, 8, BW), f32),
            pltpu.VMEM((2, 4, 18, 8, BW), f32),
            pltpu.VMEM((BLOCKS, ITERS + 1, BH, BW), f32),
            pltpu.VMEM((ENTRIES, BW), f32),
            pltpu.VMEM((DEVICES, 1, BW), f32),
            pltpu.VMEM((8, BW), i32),
            pltpu.SMEM((8, BW), i32),
            pltpu.SemaphoreType.REGULAR,
            pltpu.SemaphoreType.REGULAR,
            pltpu.SemaphoreType.REGULAR,
            pltpu.SemaphoreType.DMA((10,)),
            pltpu.SemaphoreType.DMA((CHUNKS,)),
            pltpu.SemaphoreType.DMA((tags,)),
            pltpu.SemaphoreType.DMA((tags,)),
        ],
        compiler_params=pltpu.CompilerParams(
            collective_id=0, has_side_effects=True, vmem_limit_bytes=32 * 2**20
        ),
        name="step",
    )(
        *(
            pltpu.with_memory_space_constraint(array, pltpu.HBM)
            for array in (
                baroclinic_map, barotropic_map, buoyancy_force, wet_levels, surface_patch,
                prior_height, land_mask, vertical_speed, diffusivity, tracers,
            )
        )
    )
    return pl.pallas_call(
        write_kernel,
        out_shape=(
            jax.ShapeDtypeStruct(tracers.shape, f32), jax.ShapeDtypeStruct(height_shape, f32)
        ),
        in_specs=[vmem, vmem],
        out_specs=(hbm, hbm),
        scratch_shapes=[pltpu.SemaphoreType.DMA((CHUNKS + 1,))],
        compiler_params=pltpu.CompilerParams(vmem_limit_bytes=2 * 2**20),
        name="write",
    )(tr, height)


def solution(mesh):
    return jax.shard_map(
        local,
        mesh=mesh,
        in_specs=(
            P(None, ("by", "bx"), None, None),
            P(None, ("by", "bx"), None),
            P(None, ("by", "bx"), None),
            P(None, ("by", "bx"), None),
            P(("by", "bx"), None),
            P(("by", "bx"), None),
            P(("by", "bx"), None),
            P(("by", "bx"), None, None),
            P(),
            P(),
        ),
        out_specs=(P(None, ("by", "bx"), None, None), P(("by", "bx"), None, None)),
        check_vma=False,
    )
```

```python
import jax
import jax.numpy as jnp
from jax import lax
from jax.experimental import pallas as pl
from jax.experimental.pallas import tpu as pltpu
from jax.sharding import PartitionSpec as P

MESH = pl.DeviceIdType.MESH
ITERS = 6
RESTORE = 0.5
SURFACE = 0.1
FACE_SCALE = 2.0
LEV, TR, BH, BW = 20, 16, 16, 128
CELLS = BH * BW
GBX, BLOCKS, NBX, NBY = 64, 4, 16, 8
LANES = 256
FACE = FACE_SCALE / LEV
SHIFTS = (0.0, 2.0, 1.0, 1.577, 0.4226, 0.1)
ALPHA_MAX = 82.0
PAIRS = [(i, j) for i in range(ITERS) for j in range(i, ITERS + 1)]
ENTRIES = 32
CHUNKS = 8
PARTS = (range(0, 1), range(1, 5), range(5, 8))
OWN_PART = ((0, 18), (18, 10))
ROW_PART = ((0, 9), (9, 9))
DEVICES = NBX * NBY
SUM_TAG = 28
FAR_FIRST = sorted(
    [(z, c, x, y) for z in range(4) for c in range(2) for x in range(4) for y in range(4)][1:],
    key=lambda o: -sum(min(k, 4 - k) for k in (o[0], o[2], o[3])),
)


def columns(tile, tr, speed_ref, diff_ref, wet_ref, patch_ref, coef):
    sl = pl.ds(pl.multiple_of(tile * 128, 128), 128)
    wet = wet_ref[:, sl]
    zero = jnp.zeros(wet.shape, jnp.float32)
    mix_above, pos_above, neg_above, ratio_above = zero, zero, zero, zero
    for k in range(LEV):
        is_wet = (wet > k).astype(jnp.float32)
        is_open = (wet > k + 1).astype(jnp.float32)
        speed = speed_ref[k, :, sl] * is_open
        pos, neg = jnp.maximum(speed, 0.0), jnp.minimum(speed, 0.0)
        mix = diff_ref[k, :, sl] * is_open
        pivot = 1.0 + mix + mix_above
        if k == 0:
            pivot = pivot + RESTORE * is_wet
        pivot = pivot - mix_above * ratio_above
        inv = 1.0 / pivot
        scale = is_wet * inv
        coef[0, k] = scale * (1.0 + neg - pos_above)
        coef[1, k] = scale * pos
        coef[2, k] = -scale * neg_above
        coef[3, k] = mix_above * inv
        ratio = mix * inv
        coef[4, k] = ratio
        if k == 0:
            coef[5, 0] = RESTORE * scale
        mix_above, pos_above, neg_above, ratio_above = mix, pos, neg, ratio
    ids = lax.broadcasted_iota(jnp.int32, (TR, 128), 0)
    for n in range(BLOCKS):

        def c(i, k):
            return coef[i, k, pl.ds(n, 1), :]

        values = []
        above, here, value = None, tr[0, n, :, sl], None
        for k in range(LEV):
            new = c(0, k) * here
            if k + 1 < LEV:
                below = tr[k + 1, n, :, sl]
                new = new + c(1, k) * below
            if k == 0:
                target = patch_ref[pl.ds(n, 1), sl] == ids
                new = new + jnp.where(target, c(5, 0), 0.0)
            else:
                new = new + c(2, k) * above + c(3, k) * value
            value = new
            values.append(value)
            above, here = here, below
        follow = values[-1]
        tr[LEV - 1, n, :, sl] = follow
        for k in range(LEV - 2, -1, -1):
            follow = values[k] + c(4, k) * follow
            tr[k, n, :, sl] = follow


def tree_sum(terms):
    while len(terms) > 1:
        pairs = [terms[k] + terms[k + 1] for k in range(0, len(terms) - 1, 2)]
        terms = pairs + terms[len(pairs) * 2 :]
    return terms[0]


def step_kernel(
    cmap_hbm, tmap_hbm, buoy_hbm, wet_hbm, patch_hbm, prior_hbm, land_hbm, speed_hbm, diff_hbm, tr_hbm,
    tr, out_ref,
    cmap, tmap, buoy_ref, wet_ref, patch_ref, prior_ref, land_ref, speed_ref, diff_ref, coef,
    depths, forces, send_own, recv_own, send_row, recv_row, basis, gram, ring,
    tab_v, tab_s, halo_sem, plane_sem, all_sem, lsem, tsem, ssem, rsem,
):
    row = lax.axis_index("by")
    me = lax.axis_index("bx")
    core = lax.rem(row, 2)
    below_row = lax.rem(row + 1, NBY)
    above_row = lax.rem(row + NBY - 1, NBY)
    step_a = 4 - 3 * core
    step_b = 1 + 3 * core
    px, py = me // 4, lax.rem(me, 4)
    a = px + core * (py - px)
    b = py + core * (px - py)

    def dev(i, j):
        return lax.rem(a + i, 4) * step_a + lax.rem(b + j, 4) * step_b

    barrier = pltpu.get_barrier_semaphore()

    def greet(**where):
        pl.semaphore_signal(barrier, inc=1, device_id=where, device_id_type=MESH)

    for i in range(1, 4):
        greet(bx=dev(i, 0))
        greet(bx=dev(0, i))
    for i in range(1, NBY):
        greet(by=lax.rem(row + i, NBY))
    greeted = 2 * 3 + NBY - 1

    local = [
        (wet_hbm, wet_ref), (prior_hbm, prior_ref), (buoy_hbm, buoy_ref), (land_hbm, land_ref),
        (cmap_hbm, cmap), (tmap_hbm, tmap),
        (speed_hbm, speed_ref), (diff_hbm, diff_ref), (patch_hbm, patch_ref),
    ]
    loads = [pltpu.make_async_copy(s, d, lsem.at[i]) for i, (s, d) in enumerate(local)]
    for load in loads[:6]:
        load.start()

    def remote(src, dst, tag, where):
        copy = pltpu.make_async_remote_copy(
            src_ref=src, dst_ref=dst, send_sem=ssem.at[tag], recv_sem=rsem.at[tag],
            device_id=where, device_id_type=MESH,
        )
        copy.start()
        return copy

    mine = a * BLOCKS
    gat = (depths, forces)

    def place_field(pair, q, value):
        for n in range(BLOCKS):
            for r in range(BH):
                gat[pair][mine + n, q, pl.ds(r, 1), :] = value[n : n + 1, r * BW : (r + 1) * BW]

    def share(pair):
        chunk = gat[pair].at[pl.ds(mine, BLOCKS)]
        return [remote(chunk, chunk, 3 * pair + i - 1, {"bx": dev(i, 0)}) for i in (2, 1, 3)]

    loads[0].wait()
    loads[1].wait()
    wet = wet_ref[...]
    place_field(0, 0, wet.astype(jnp.float32))
    place_field(0, 1, prior_ref[...])
    pl.semaphore_wait(barrier, greeted)
    first = [share(0)]
    for to in (below_row, above_row):
        pl.semaphore_signal(halo_sem, inc=1, device_id={"by": to}, device_id_type=MESH)
    for i in range(1, 4):
        pl.semaphore_signal(plane_sem, inc=1, device_id={"bx": dev(0, i)}, device_id_type=MESH)

    loads[2].wait()
    loads[3].wait()
    total = jnp.zeros(wet.shape, jnp.float32)
    for k in range(LEV):
        total = total + jnp.where(wet > k, buoy_ref[k].astype(jnp.float32), 0.0)
    place_field(1, 0, total)
    for n in range(BLOCKS):
        gat[1][mine + n, 1] = land_ref[n].astype(jnp.float32)
    first.append(share(1))

    for load in loads[6:]:
        load.start()
    width = CELLS // CHUNKS
    streams = []
    for i in range(CHUNKS):
        part = (slice(None), slice(None), slice(None), pl.ds(i * width, width))
        streams.append(pltpu.make_async_copy(tr_hbm.at[part], tr.at[part], tsem.at[i]))
        streams[i].start()

    lane = lax.broadcasted_iota(jnp.int32, (1, BW), 1)
    sources = ((row, core, b), (above_row, 1 - core, a), (below_row, 1 - core, a))

    def fill(s, tabs):
        tabs = list(tabs)
        sx, sy, slot = s // 16, lax.rem(s // 4, 4), lax.rem(s, 4)
        for r, (which, its_core, its_b) in enumerate(sources):
            sa = sx + its_core * (sy - sx)
            sb = sy + its_core * (sx - sy)
            offset = lax.rem(its_b - sb + 4, 4)
            for kind, ref in enumerate((cmap, tmap)):
                hit = lane == lax.rem(ref[which * GBX + s], GBX)
                if r == 0:
                    tabs[kind] = jnp.where(hit, sa * BLOCKS + slot, tabs[kind])
                tabs[2 + 2 * r + kind] = jnp.where(hit, offset, tabs[2 + 2 * r + kind])
        return tuple(tabs)

    loads[4].wait()
    loads[5].wait()
    tabs = lax.fori_loop(0, GBX, fill, tuple(jnp.zeros((1, BW), jnp.int32) for _ in range(8)))
    for i in range(8):
        tab_v[pl.ds(i, 1), :] = tabs[i]
    load_tab = pltpu.make_async_copy(tab_v, tab_s, lsem.at[9])
    load_tab.start()

    pl.semaphore_wait(plane_sem, 3)
    for i in range(1, NBY):
        pl.semaphore_signal(
            all_sem, inc=1, device_id={"by": lax.rem(row + i, NBY)}, device_id_type=MESH
        )
    def run_columns(part):
        if part == 0:
            for load in loads[6:]:
                load.wait()
        per = width // 128
        for i in PARTS[part]:
            streams[i].wait()
        chunks = PARTS[part]

        def body(t, carry):
            columns(t, tr, speed_ref, diff_ref, wet_ref, patch_ref, coef)
            return carry

        lax.fori_loop(chunks.start * per, chunks.stop * per, body, 0)

    load_tab.wait()

    lane8 = lax.broadcasted_iota(jnp.int32, (8, BW), 1)
    window_of = lane8 // 8

    def window(q, n, side):
        return q * 8 + 2 * n + side

    def kind_of(pair, q):
        return 1 if (pair, q) == (1, 1) else 0

    def turned(v, shift):
        return pltpu.roll(v, shift % BW, 1) if shift % BW else v

    def pack(dst, pair, role, i):
        its_row = (row, below_row, above_row)[role]
        base = its_row * GBX + dev(0, i) * BLOCKS
        place = {}
        for n in range(BLOCKS):
            g = lax.rem(tmap[base + n], GBX)
            for side, shift in ((0, 1), (1, GBX - 1), (2, 0)):
                at = lax.rem(g + shift, GBX)
                for kind in range(1 + pair):
                    place[kind, n, side] = tab_s[kind, at]
        halves = ((0, 1), (1,), (0,))[role]
        t = (OWN_PART if role == 0 else ROW_PART)[pair][0]
        for n in range(BLOCKS):
            for q in range(1 if (role, pair) == (0, 1) else 2):
                for h in halves:
                    dst[t] = gat[pair][place[kind_of(pair, q), n, 2], q, pl.ds(8 * h, 8), :]
                    t += 1
        for h in halves:
            tile = jnp.zeros((8, BW), jnp.float32)
            for q in range(2):
                for n in range(BLOCKS):
                    for side in range(2):
                        w = window(q, n, side)
                        v = gat[pair][place[kind_of(pair, q), n, side], q, pl.ds(8 * h, 8), :]
                        v = turned(v, 8 * w + (8 if side else 0))
                        tile = jnp.where(window_of == w, v, tile)
            dst[t] = tile
            t += 1

    pl.semaphore_wait(halo_sem, 2)
    second = []
    for pair in range(2):
        for copy in first[pair]:
            copy.wait_recv()
        row_part, own_part = pl.ds(*ROW_PART[pair]), pl.ds(*OWN_PART[pair])
        for i in (2, 1, 3, 0):
            for d in range(2):
                pack(send_row.at[d, i], pair, 1 + d, i)
                to = below_row if d == 0 else above_row
                second.append(
                    remote(
                        send_row.at[d, i, row_part], recv_row.at[d, i, row_part],
                        12 + 8 * pair + 4 * d + i, {"by": to, "bx": dev(0, i)},
                    )
                )
            if i:
                pack(send_own.at[i - 1], pair, 0, i)
                second.append(
                    remote(
                        send_own.at[i - 1, own_part], recv_own.at[i, own_part],
                        5 + 3 * pair + i, {"bx": dev(0, i)},
                    )
                )
            else:
                pack(recv_own.at[0], pair, 0, 0)
        if pair == 0:
            run_columns(0)
    run_columns(1)
    for copy in second:
        copy.wait_recv()

    has_north = (row > 0).astype(jnp.float32)
    has_south = (row < NBY - 1).astype(jnp.float32)
    acc = [None] * len(PAIRS)
    for n in range(BLOCKS):
        g = lax.rem(tmap[row * GBX + me * BLOCKS + n], GBX)
        around = [lax.rem(g + shift, GBX) for shift in (1, GBX - 1, 0)]
        came = {
            (src, kind, side): tab_s[2 + 2 * src + kind, around[side]]
            for src in range(3) for kind in range(2) for side in range(3)
        }

        def beside(buf, src, pair, q, at):
            kind = kind_of(pair, q)
            east = turned(buf[came[src, kind, 0], at], BW - 8 * window(q, n, 0))
            west = turned(buf[came[src, kind, 1], at], BW - 8 - 8 * window(q, n, 1))
            return jnp.where(lane8 < 8, east, jnp.where(lane8 >= BW - 8, west, 0.0))

        whole = {}
        for pair in range(2):
            row_base, own_base = ROW_PART[pair][0], OWN_PART[pair][0]
            for q in range(2):
                kind = kind_of(pair, q)
                ends = []
                for d in range(2):
                    buf = recv_row.at[d]
                    middle = buf[came[1 + d, kind, 2], row_base + n * 2 + q]
                    side = beside(buf, 1 + d, pair, q, row_base + 8)
                    end = jnp.concatenate([middle, side], axis=1)
                    if kind:
                        end = end * (has_north if d == 0 else has_south)
                    ends.append(end)
                parts = [ends[0]]
                for h in range(2):
                    if kind:
                        middle = gat[1][mine + n, 1, pl.ds(8 * h, 8), :]
                    elif pair:
                        middle = recv_own[came[0, 0, 2], own_base + n * 2 + h]
                    else:
                        middle = recv_own[came[0, 0, 2], own_base + (n * 2 + q) * 2 + h]
                    edges = own_base + (8 if pair else 16)
                    side = beside(recv_own, 0, pair, q, edges + h)
                    parts.append(jnp.concatenate([middle, side], axis=1))
                parts.append(ends[1])
                whole[pair, q] = jnp.concatenate(parts, axis=0)
        depth, prior, force, ocean = whole[0, 0], whole[0, 1], whole[1, 0], whole[1, 1]
        rows = BH + 16

        def east(v):
            return pltpu.roll(v, LANES - 1, 1)

        def west(v):
            return pltpu.roll(v, 1, 1)

        def south_of(v):
            return pltpu.roll(v, rows - 1, 0)

        def north_of(v):
            return pltpu.roll(v, 1, 0)

        face_e = FACE * jnp.minimum(depth, east(depth)) * ocean * east(ocean)
        face_s = FACE * jnp.minimum(depth, south_of(depth)) * ocean * south_of(ocean)
        face_w, face_n = west(face_e), north_of(face_s)
        centre = SURFACE * ocean + (1.0 - ocean)
        diag = centre + face_e + face_w + face_s + face_n
        inv = 1.0 / diag
        centre, face_e, face_w = centre * inv, face_e * inv, face_w * inv
        face_s, face_n = face_s * inv, face_n * inv

        def scaled(v):
            out = centre * v + face_e * (v - east(v)) + face_w * (v - west(v))
            return out + face_s * (v - south_of(v)) + face_n * (v - north_of(v))

        def own(v):
            return v[8 : 8 + BH, :BW]

        guess = ocean * prior
        u = ocean * force * inv - scaled(guess)
        weight = own(diag)
        basis[n, ITERS] = own(guess)
        mine_of, weighted = [], []
        for k in range(ITERS + 1):
            mine_of.append(own(u))
            if k < ITERS:
                basis[n, k] = mine_of[k]
                weighted.append(weight * mine_of[k])
                image = scaled(u)
                u = image - SHIFTS[k] * u if SHIFTS[k] else image
        for e, (i, j) in enumerate(PAIRS):
            prod = weighted[i] * mine_of[j]
            prod = prod[:8] + prod[8:]
            acc[e] = prod if acc[e] is None else acc[e] + prod

    for e in range(len(PAIRS)):
        gram[pl.ds(e, 1), :] = jnp.sum(acc[e], axis=0, keepdims=True)
    gram[pl.ds(len(PAIRS), ENTRIES - len(PAIRS)), :] = jnp.zeros(
        (ENTRIES - len(PAIRS), BW), jnp.float32
    )
    on_diag = lax.broadcasted_iota(jnp.int32, (ENTRIES, BW), 0) == lax.broadcasted_iota(
        jnp.int32, (ENTRIES, BW), 1
    )
    placed = jnp.where(on_diag, jnp.sum(gram[...], axis=1, keepdims=True), 0.0)
    packed = placed[0:8] + placed[8:16] + placed[16:24] + placed[24:32]

    pl.semaphore_wait(all_sem, NBY - 1)
    flat = row * NBX + me
    ring[flat] = jnp.sum(packed, axis=0, keepdims=True)
    for dz, dc, dx, dy in FAR_FIRST:
        to_row = lax.rem(row // 2 + dz, 4) * 2 + lax.rem(core + dc, 2)
        to = lax.rem(px + dx, 4) * 4 + lax.rem(py + dy, 4)
        remote(ring.at[flat], ring.at[flat], SUM_TAG, {"by": to_row, "bx": to})
    run_columns(2)
    others = ring.at[pl.ds(0, DEVICES - 1)]
    pltpu.make_async_copy(others, others, rsem.at[SUM_TAG]).wait()
    line = tree_sum([ring[k] for k in range(DEVICES)])
    spread = jnp.sum(jnp.where(on_diag, line, 0.0), axis=1, keepdims=True)
    spread = jnp.broadcast_to(spread, (ENTRIES, BW))
    g = {}
    for e, (i, j) in enumerate(PAIRS):
        g[i, j] = g[j, i] = spread[e : e + 1]

    def form(left, right):
        inner = [tree_sum([g[i, j] * vj for j, vj in enumerate(right)]) for i in range(len(left))]
        return tree_sum([vi * w for vi, w in zip(left, inner)])

    one = jnp.ones((1, BW), jnp.float32)
    zero = jnp.zeros((1, BW), jnp.float32)
    p, z = [one], [one]
    x = [zero] * ITERS
    rz = g[0, 0]
    for it in range(ITERS):
        y = [SHIFTS[k] * p[k] if SHIFTS[k] else zero for k in range(it + 1)] + [zero]
        for k in range(it + 1):
            y[k + 1] = y[k + 1] + p[k]
        pq = form(p, y)
        live = jnp.logical_and(rz > 0.0, pq > 0.0)
        alpha = jnp.where(live, rz, 0.0) / jnp.where(live, pq, 1.0)
        alpha = jnp.minimum(alpha, ALPHA_MAX)
        for k in range(it + 1):
            x[k] = x[k] + alpha * p[k]
        if it + 1 < ITERS:
            z = [zk - alpha * yk for zk, yk in zip(z + [zero], y)]
            rz_new = jnp.maximum(form(z, z), 0.0)
            beta = jnp.where(live, rz_new, 0.0) / jnp.where(live, rz, 1.0)
            p = [zk + beta * pk for zk, pk in zip(z, p + [zero])]
            rz = rz_new
    pltpu.make_async_copy(others, others, ssem.at[SUM_TAG]).wait()
    for copy in first[0] + first[1] + second:
        copy.wait_send()
    for n in range(BLOCKS):
        height = basis[n, ITERS]
        for k in range(ITERS):
            height = height + x[k] * basis[n, k]
        out_ref[n] = height


def write_kernel(tr, height, tr_out, height_out, sem):
    width = CELLS // CHUNKS
    copies = [pltpu.make_async_copy(height, height_out, sem.at[CHUNKS])]
    for i in range(CHUNKS):
        part = (slice(None), slice(None), slice(None), pl.ds(i * width, width))
        copies.append(pltpu.make_async_copy(tr.at[part], tr_out.at[part], sem.at[i]))
    for copy in copies:
        copy.start()
    for copy in copies:
        copy.wait()


def local(
    tracers, vertical_speed, diffusivity, buoyancy_force, wet_levels, surface_patch,
    prior_height, land_mask, baroclinic_map, barotropic_map,
):
    f32, i32 = jnp.float32, jnp.int32
    vmem = pl.BlockSpec(memory_space=pltpu.VMEM)
    hbm = pl.BlockSpec(memory_space=pltpu.HBM)
    tags = SUM_TAG + 1
    height_shape = (BLOCKS, BH, BW)
    tr, height = pl.pallas_call(
        step_kernel,
        out_shape=(pltpu.VMEM(tracers.shape, f32), pltpu.VMEM(height_shape, f32)),
        in_specs=[hbm] * 10,
        out_specs=(vmem, vmem),
        scratch_shapes=[
            pltpu.SMEM((NBY * GBX,), i32),
            pltpu.SMEM((NBY * GBX,), i32),
            pltpu.VMEM((LEV, BLOCKS, CELLS), jnp.bfloat16),
            pltpu.VMEM((BLOCKS, CELLS), i32),
            pltpu.VMEM((BLOCKS, CELLS), i32),
            pltpu.VMEM((BLOCKS, CELLS), f32),
            pltpu.VMEM(height_shape, i32),
            pltpu.VMEM((LEV, BLOCKS, CELLS), f32),
            pltpu.VMEM((LEV, BLOCKS, CELLS), f32),
            pltpu.VMEM((6, LEV, BLOCKS, 128), f32),
            pltpu.VMEM((4 * BLOCKS, 2, BH, BW), f32),
            pltpu.VMEM((4 * BLOCKS, 2, BH, BW), f32),
            pltpu.VMEM((3, 28, 8, BW), f32),
            pltpu.VMEM((4, 28, 8, BW), f32),
            pltpu.VMEM((2, 4, 18, 8, BW), f32),
            pltpu.VMEM((2, 4, 18, 8, BW), f32),
            pltpu.VMEM((BLOCKS, ITERS + 1, BH, BW), f32),
            pltpu.VMEM((ENTRIES, BW), f32),
            pltpu.VMEM((DEVICES, 1, BW), f32),
            pltpu.VMEM((8, BW), i32),
            pltpu.SMEM((8, BW), i32),
            pltpu.SemaphoreType.REGULAR,
            pltpu.SemaphoreType.REGULAR,
            pltpu.SemaphoreType.REGULAR,
            pltpu.SemaphoreType.DMA((10,)),
            pltpu.SemaphoreType.DMA((CHUNKS,)),
            pltpu.SemaphoreType.DMA((tags,)),
            pltpu.SemaphoreType.DMA((tags,)),
        ],
        compiler_params=pltpu.CompilerParams(
            collective_id=0, has_side_effects=True, vmem_limit_bytes=32 * 2**20
        ),
        name="step",
    )(
        *(
            pltpu.with_memory_space_constraint(array, pltpu.HBM)
            for array in (
                baroclinic_map, barotropic_map, buoyancy_force, wet_levels, surface_patch,
                prior_height, land_mask, vertical_speed, diffusivity, tracers,
            )
        )
    )
    return pl.pallas_call(
        write_kernel,
        out_shape=(
            jax.ShapeDtypeStruct(tracers.shape, f32), jax.ShapeDtypeStruct(height_shape, f32)
        ),
        in_specs=[vmem, vmem],
        out_specs=(hbm, hbm),
        scratch_shapes=[pltpu.SemaphoreType.DMA((CHUNKS + 1,))],
        compiler_params=pltpu.CompilerParams(vmem_limit_bytes=2 * 2**20),
        name="write",
    )(tr, height)


def solution(mesh):
    return jax.shard_map(
        local,
        mesh=mesh,
        in_specs=(
            P(None, ("by", "bx"), None, None),
            P(None, ("by", "bx"), None),
            P(None, ("by", "bx"), None),
            P(None, ("by", "bx"), None),
            P(("by", "bx"), None),
            P(("by", "bx"), None),
            P(("by", "bx"), None),
            P(("by", "bx"), None, None),
            P(),
            P(),
        ),
        out_specs=(P(None, ("by", "bx"), None, None), P(("by", "bx"), None, None)),
        check_vma=False,
    )
```

```python
import jax
import jax.numpy as jnp
from jax import lax
from jax.experimental import pallas as pl
from jax.experimental.pallas import tpu as pltpu
from jax.sharding import PartitionSpec as P

MESH = pl.DeviceIdType.MESH
ITERS = 6
RESTORE = 0.5
SURFACE = 0.1
FACE_SCALE = 2.0
LEV, TR, BH, BW = 20, 16, 16, 128
CELLS = BH * BW
GBX, BLOCKS, NBX, NBY = 64, 4, 16, 8
LANES = 256
FACE = FACE_SCALE / LEV
SHIFTS = (0.0, 2.0, 1.0, 1.577, 0.4226, 0.1)
ALPHA_MAX = 82.0
PAIRS = [(i, j) for i in range(ITERS) for j in range(i, ITERS + 1)]
ENTRIES = 32
CHUNKS = 8
PARTS = (range(0, 0), range(0, 4), range(4, 8))
OWN_PART = ((0, 18), (18, 10))
ROW_PART = ((0, 9), (9, 9))
DEVICES = NBX * NBY
SUM_TAG = 28
FAR_FIRST = sorted(
    [(z, c, x, y) for z in range(4) for c in range(2) for x in range(4) for y in range(4)][1:],
    key=lambda o: -sum(min(k, 4 - k) for k in (o[0], o[2], o[3])),
)


def columns(tile, tr, speed_ref, diff_ref, wet_ref, patch_ref, coef):
    sl = pl.ds(pl.multiple_of(tile * 128, 128), 128)
    wet = wet_ref[:, sl]
    zero = jnp.zeros(wet.shape, jnp.float32)
    mix_above, pos_above, neg_above, ratio_above = zero, zero, zero, zero
    for k in range(LEV):
        is_wet = (wet > k).astype(jnp.float32)
        is_open = (wet > k + 1).astype(jnp.float32)
        speed = speed_ref[k, :, sl] * is_open
        pos, neg = jnp.maximum(speed, 0.0), jnp.minimum(speed, 0.0)
        mix = diff_ref[k, :, sl] * is_open
        pivot = 1.0 + mix + mix_above
        if k == 0:
            pivot = pivot + RESTORE * is_wet
        pivot = pivot - mix_above * ratio_above
        inv = 1.0 / pivot
        scale = is_wet * inv
        coef[0, k] = scale * (1.0 + neg - pos_above)
        coef[1, k] = scale * pos
        coef[2, k] = -scale * neg_above
        coef[3, k] = mix_above * inv
        ratio = mix * inv
        coef[4, k] = ratio
        if k == 0:
            coef[5, 0] = RESTORE * scale
        mix_above, pos_above, neg_above, ratio_above = mix, pos, neg, ratio
    ids = lax.broadcasted_iota(jnp.int32, (TR, 128), 0)
    for n in range(BLOCKS):

        def c(i, k):
            return coef[i, k, pl.ds(n, 1), :]

        values = []
        above, here, value = None, tr[0, n, :, sl], None
        for k in range(LEV):
            new = c(0, k) * here
            if k + 1 < LEV:
                below = tr[k + 1, n, :, sl]
                new = new + c(1, k) * below
            if k == 0:
                target = patch_ref[pl.ds(n, 1), sl] == ids
                new = new + jnp.where(target, c(5, 0), 0.0)
            else:
                new = new + c(2, k) * above + c(3, k) * value
            value = new
            values.append(value)
            above, here = here, below
        follow = values[-1]
        tr[LEV - 1, n, :, sl] = follow
        for k in range(LEV - 2, -1, -1):
            follow = values[k] + c(4, k) * follow
            tr[k, n, :, sl] = follow


def step_kernel(
    cmap_hbm, tmap_hbm, buoy_hbm, wet_hbm, patch_hbm, prior_hbm, land_hbm, speed_hbm, diff_hbm, tr_hbm,
    tr, out_ref,
    cmap, tmap, buoy_ref, wet_ref, patch_ref, prior_ref, land_ref, speed_ref, diff_ref, coef,
    depths, forces, send_own, recv_own, send_row, recv_row, basis, gram, ring,
    tab_v, tab_s, halo_sem, plane_sem, all_sem, lsem, tsem, ssem, rsem,
):
    row = lax.axis_index("by")
    me = lax.axis_index("bx")
    core = lax.rem(row, 2)
    below_row = lax.rem(row + 1, NBY)
    above_row = lax.rem(row + NBY - 1, NBY)
    step_a = 4 - 3 * core
    step_b = 1 + 3 * core
    px, py = me // 4, lax.rem(me, 4)
    a = px + core * (py - px)
    b = py + core * (px - py)

    def dev(i, j):
        return lax.rem(a + i, 4) * step_a + lax.rem(b + j, 4) * step_b

    barrier = pltpu.get_barrier_semaphore()

    def greet(**where):
        pl.semaphore_signal(barrier, inc=1, device_id=where, device_id_type=MESH)

    for i in range(1, 4):
        greet(bx=dev(i, 0))
        greet(bx=dev(0, i))
    for i in range(1, NBY):
        greet(by=lax.rem(row + i, NBY))
    greeted = 2 * 3 + NBY - 1

    local = [
        (wet_hbm, wet_ref), (prior_hbm, prior_ref), (buoy_hbm, buoy_ref), (land_hbm, land_ref),
        (cmap_hbm, cmap), (tmap_hbm, tmap),
        (speed_hbm, speed_ref), (diff_hbm, diff_ref), (patch_hbm, patch_ref),
    ]
    loads = [pltpu.make_async_copy(s, d, lsem.at[i]) for i, (s, d) in enumerate(local)]
    for load in loads[:6]:
        load.start()

    def remote(src, dst, tag, where):
        copy = pltpu.make_async_remote_copy(
            src_ref=src, dst_ref=dst, send_sem=ssem.at[tag], recv_sem=rsem.at[tag],
            device_id=where, device_id_type=MESH,
        )
        copy.start()
        return copy

    mine = a * BLOCKS
    gat = (depths, forces)

    def place_field(pair, q, value):
        for n in range(BLOCKS):
            for r in range(BH):
                gat[pair][mine + n, q, pl.ds(r, 1), :] = value[n : n + 1, r * BW : (r + 1) * BW]

    def share(pair):
        chunk = gat[pair].at[pl.ds(mine, BLOCKS)]
        return [remote(chunk, chunk, 3 * pair + i - 1, {"bx": dev(i, 0)}) for i in (2, 1, 3)]

    loads[0].wait()
    loads[1].wait()
    wet = wet_ref[...]
    place_field(0, 0, wet.astype(jnp.float32))
    place_field(0, 1, prior_ref[...])
    pl.semaphore_wait(barrier, greeted)
    first = [share(0)]
    for to in (below_row, above_row):
        pl.semaphore_signal(halo_sem, inc=1, device_id={"by": to}, device_id_type=MESH)
    for i in range(1, 4):
        pl.semaphore_signal(plane_sem, inc=1, device_id={"bx": dev(0, i)}, device_id_type=MESH)

    loads[2].wait()
    loads[3].wait()
    total = jnp.zeros(wet.shape, jnp.float32)
    for k in range(LEV):
        total = total + jnp.where(wet > k, buoy_ref[k].astype(jnp.float32), 0.0)
    place_field(1, 0, total)
    for n in range(BLOCKS):
        gat[1][mine + n, 1] = land_ref[n].astype(jnp.float32)
    first.append(share(1))

    for load in loads[6:]:
        load.start()
    width = CELLS // CHUNKS
    streams = []
    for i in range(CHUNKS):
        part = (slice(None), slice(None), slice(None), pl.ds(i * width, width))
        streams.append(pltpu.make_async_copy(tr_hbm.at[part], tr.at[part], tsem.at[i]))
        streams[i].start()

    lane = lax.broadcasted_iota(jnp.int32, (1, BW), 1)
    sources = ((row, core, b), (above_row, 1 - core, a), (below_row, 1 - core, a))

    def fill(s, tabs):
        tabs = list(tabs)
        sx, sy, slot = s // 16, lax.rem(s // 4, 4), lax.rem(s, 4)
        for r, (which, its_core, its_b) in enumerate(sources):
            sa = sx + its_core * (sy - sx)
            sb = sy + its_core * (sx - sy)
            offset = lax.rem(its_b - sb + 4, 4)
            for kind, ref in enumerate((cmap, tmap)):
                hit = lane == lax.rem(ref[which * GBX + s], GBX)
                if r == 0:
                    tabs[kind] = jnp.where(hit, sa * BLOCKS + slot, tabs[kind])
                tabs[2 + 2 * r + kind] = jnp.where(hit, offset, tabs[2 + 2 * r + kind])
        return tuple(tabs)

    loads[4].wait()
    loads[5].wait()
    tabs = lax.fori_loop(0, GBX, fill, tuple(jnp.zeros((1, BW), jnp.int32) for _ in range(8)))
    for i in range(8):
        tab_v[pl.ds(i, 1), :] = tabs[i]
    load_tab = pltpu.make_async_copy(tab_v, tab_s, lsem.at[9])
    load_tab.start()

    pl.semaphore_wait(plane_sem, 3)
    for i in range(1, NBY):
        pl.semaphore_signal(
            all_sem, inc=1, device_id={"by": lax.rem(row + i, NBY)}, device_id_type=MESH
        )
    def run_columns(part):
        if part == 0:
            for load in loads[6:]:
                load.wait()
        per = width // 128
        for i in PARTS[part]:
            streams[i].wait()
        chunks = PARTS[part]

        def body(t, carry):
            columns(t, tr, speed_ref, diff_ref, wet_ref, patch_ref, coef)
            return carry

        lax.fori_loop(chunks.start * per, chunks.stop * per, body, 0)

    load_tab.wait()

    lane8 = lax.broadcasted_iota(jnp.int32, (8, BW), 1)
    window_of = lane8 // 8

    def window(q, n, side):
        return q * 8 + 2 * n + side

    def kind_of(pair, q):
        return 1 if (pair, q) == (1, 1) else 0

    def turned(v, shift):
        return pltpu.roll(v, shift % BW, 1) if shift % BW else v

    def pack(dst, pair, role, i):
        its_row = (row, below_row, above_row)[role]
        base = its_row * GBX + dev(0, i) * BLOCKS
        place = {}
        for n in range(BLOCKS):
            g = lax.rem(tmap[base + n], GBX)
            for side, shift in ((0, 1), (1, GBX - 1), (2, 0)):
                at = lax.rem(g + shift, GBX)
                for kind in range(1 + pair):
                    place[kind, n, side] = tab_s[kind, at]
        halves = ((0, 1), (1,), (0,))[role]
        t = (OWN_PART if role == 0 else ROW_PART)[pair][0]
        for n in range(BLOCKS):
            for q in range(1 if (role, pair) == (0, 1) else 2):
                for h in halves:
                    dst[t] = gat[pair][place[kind_of(pair, q), n, 2], q, pl.ds(8 * h, 8), :]
                    t += 1
        for h in halves:
            tile = jnp.zeros((8, BW), jnp.float32)
            for q in range(2):
                for n in range(BLOCKS):
                    for side in range(2):
                        w = window(q, n, side)
                        v = gat[pair][place[kind_of(pair, q), n, side], q, pl.ds(8 * h, 8), :]
                        v = turned(v, 8 * w + (8 if side else 0))
                        tile = jnp.where(window_of == w, v, tile)
            dst[t] = tile
            t += 1

    pl.semaphore_wait(halo_sem, 2)
    second = []
    for pair in range(2):
        for copy in first[pair]:
            copy.wait_recv()
        row_part, own_part = pl.ds(*ROW_PART[pair]), pl.ds(*OWN_PART[pair])
        for i in (2, 1, 3, 0):
            for d in range(2):
                pack(send_row.at[d, i], pair, 1 + d, i)
                to = below_row if d == 0 else above_row
                second.append(
                    remote(
                        send_row.at[d, i, row_part], recv_row.at[d, i, row_part],
                        12 + 8 * pair + 4 * d + i, {"by": to, "bx": dev(0, i)},
                    )
                )
            if i:
                pack(send_own.at[i - 1], pair, 0, i)
                second.append(
                    remote(
                        send_own.at[i - 1, own_part], recv_own.at[i, own_part],
                        5 + 3 * pair + i, {"bx": dev(0, i)},
                    )
                )
            else:
                pack(recv_own.at[0], pair, 0, 0)
        if pair == 0:
            run_columns(0)
    run_columns(1)
    for copy in second:
        copy.wait_recv()

    has_north = (row > 0).astype(jnp.float32)
    has_south = (row < NBY - 1).astype(jnp.float32)
    acc = [None] * len(PAIRS)
    for n in range(BLOCKS):
        g = lax.rem(tmap[row * GBX + me * BLOCKS + n], GBX)
        around = [lax.rem(g + shift, GBX) for shift in (1, GBX - 1, 0)]
        came = {
            (src, kind, side): tab_s[2 + 2 * src + kind, around[side]]
            for src in range(3) for kind in range(2) for side in range(3)
        }

        def beside(buf, src, pair, q, at):
            kind = kind_of(pair, q)
            east = turned(buf[came[src, kind, 0], at], BW - 8 * window(q, n, 0))
            west = turned(buf[came[src, kind, 1], at], BW - 8 - 8 * window(q, n, 1))
            return jnp.where(lane8 < 8, east, jnp.where(lane8 >= BW - 8, west, 0.0))

        whole = {}
        for pair in range(2):
            row_base, own_base = ROW_PART[pair][0], OWN_PART[pair][0]
            for q in range(2):
                kind = kind_of(pair, q)
                ends = []
                for d in range(2):
                    buf = recv_row.at[d]
                    middle = buf[came[1 + d, kind, 2], row_base + n * 2 + q]
                    side = beside(buf, 1 + d, pair, q, row_base + 8)
                    end = jnp.concatenate([middle, side], axis=1)
                    if kind:
                        end = end * (has_north if d == 0 else has_south)
                    ends.append(end)
                parts = [ends[0]]
                for h in range(2):
                    if kind:
                        middle = gat[1][mine + n, 1, pl.ds(8 * h, 8), :]
                    elif pair:
                        middle = recv_own[came[0, 0, 2], own_base + n * 2 + h]
                    else:
                        middle = recv_own[came[0, 0, 2], own_base + (n * 2 + q) * 2 + h]
                    edges = own_base + (8 if pair else 16)
                    side = beside(recv_own, 0, pair, q, edges + h)
                    parts.append(jnp.concatenate([middle, side], axis=1))
                parts.append(ends[1])
                whole[pair, q] = jnp.concatenate(parts, axis=0)
        depth, prior, force, ocean = whole[0, 0], whole[0, 1], whole[1, 0], whole[1, 1]
        rows = BH + 16

        def east(v):
            return pltpu.roll(v, LANES - 1, 1)

        def west(v):
            return pltpu.roll(v, 1, 1)

        def south_of(v):
            return pltpu.roll(v, rows - 1, 0)

        def north_of(v):
            return pltpu.roll(v, 1, 0)

        face_e = FACE * jnp.minimum(depth, east(depth)) * ocean * east(ocean)
        face_s = FACE * jnp.minimum(depth, south_of(depth)) * ocean * south_of(ocean)
        face_w, face_n = west(face_e), north_of(face_s)
        centre = SURFACE * ocean + (1.0 - ocean)
        diag = centre + face_e + face_w + face_s + face_n
        inv = 1.0 / diag
        centre, face_e, face_w = centre * inv, face_e * inv, face_w * inv
        face_s, face_n = face_s * inv, face_n * inv

        def scaled(v):
            out = centre * v + face_e * (v - east(v)) + face_w * (v - west(v))
            return out + face_s * (v - south_of(v)) + face_n * (v - north_of(v))

        def own(v):
            return v[8 : 8 + BH, :BW]

        guess = ocean * prior
        u = ocean * force * inv - scaled(guess)
        weight = own(diag)
        basis[n, ITERS] = own(guess)
        mine_of, weighted = [], []
        for k in range(ITERS + 1):
            mine_of.append(own(u))
            if k < ITERS:
                basis[n, k] = mine_of[k]
                weighted.append(weight * mine_of[k])
                image = scaled(u)
                u = image - SHIFTS[k] * u if SHIFTS[k] else image
        for e, (i, j) in enumerate(PAIRS):
            prod = weighted[i] * mine_of[j]
            prod = prod[:8] + prod[8:]
            acc[e] = prod if acc[e] is None else acc[e] + prod

    for e in range(len(PAIRS)):
        gram[pl.ds(e, 1), :] = jnp.sum(acc[e], axis=0, keepdims=True)
    gram[pl.ds(len(PAIRS), ENTRIES - len(PAIRS)), :] = jnp.zeros(
        (ENTRIES - len(PAIRS), BW), jnp.float32
    )
    on_diag = lax.broadcasted_iota(jnp.int32, (ENTRIES, BW), 0) == lax.broadcasted_iota(
        jnp.int32, (ENTRIES, BW), 1
    )
    placed = jnp.where(on_diag, jnp.sum(gram[...], axis=1, keepdims=True), 0.0)
    packed = placed[0:8] + placed[8:16] + placed[16:24] + placed[24:32]

    pl.semaphore_wait(all_sem, NBY - 1)
    flat = row * NBX + me
    ring[flat] = jnp.sum(packed, axis=0, keepdims=True)
    for dz, dc, dx, dy in FAR_FIRST:
        to_row = lax.rem(row // 2 + dz, 4) * 2 + lax.rem(core + dc, 2)
        to = lax.rem(px + dx, 4) * 4 + lax.rem(py + dy, 4)
        remote(ring.at[flat], ring.at[flat], SUM_TAG, {"by": to_row, "bx": to})
    run_columns(2)
    others = ring.at[pl.ds(0, DEVICES - 1)]
    pltpu.make_async_copy(others, others, rsem.at[SUM_TAG]).wait()
    line = jnp.sum(ring[...], axis=0)
    spread = jnp.sum(jnp.where(on_diag, line, 0.0), axis=1, keepdims=True)
    spread = jnp.broadcast_to(spread, (ENTRIES, BW))
    g = {}
    for e, (i, j) in enumerate(PAIRS):
        g[i, j] = g[j, i] = spread[e : e + 1]

    def form(left, right):
        out = None
        for i, vi in enumerate(left):
            inner = None
            for j, vj in enumerate(right):
                term = g[i, j] * vj
                inner = term if inner is None else inner + term
            out = vi * inner if out is None else out + vi * inner
        return out

    one = jnp.ones((1, BW), jnp.float32)
    zero = jnp.zeros((1, BW), jnp.float32)
    p, z = [one], [one]
    x = [zero] * ITERS
    rz = g[0, 0]
    for it in range(ITERS):
        y = [SHIFTS[k] * p[k] if SHIFTS[k] else zero for k in range(it + 1)] + [zero]
        for k in range(it + 1):
            y[k + 1] = y[k + 1] + p[k]
        pq = form(p, y)
        live = jnp.logical_and(rz > 0.0, pq > 0.0)
        alpha = jnp.where(live, rz, 0.0) / jnp.where(live, pq, 1.0)
        alpha = jnp.minimum(alpha, ALPHA_MAX)
        for k in range(it + 1):
            x[k] = x[k] + alpha * p[k]
        if it + 1 < ITERS:
            z = [zk - alpha * yk for zk, yk in zip(z + [zero], y)]
            rz_new = jnp.maximum(form(z, z), 0.0)
            beta = jnp.where(live, rz_new, 0.0) / jnp.where(live, rz, 1.0)
            p = [zk + beta * pk for zk, pk in zip(z, p + [zero])]
            rz = rz_new
    pltpu.make_async_copy(others, others, ssem.at[SUM_TAG]).wait()
    for copy in first[0] + first[1] + second:
        copy.wait_send()
    for n in range(BLOCKS):
        height = basis[n, ITERS]
        for k in range(ITERS):
            height = height + x[k] * basis[n, k]
        out_ref[n] = height


def write_kernel(tr, height, tr_out, height_out, sem):
    width = CELLS // CHUNKS
    copies = [pltpu.make_async_copy(height, height_out, sem.at[CHUNKS])]
    for i in range(CHUNKS):
        part = (slice(None), slice(None), slice(None), pl.ds(i * width, width))
        copies.append(pltpu.make_async_copy(tr.at[part], tr_out.at[part], sem.at[i]))
    for copy in copies:
        copy.start()
    for copy in copies:
        copy.wait()


def local(
    tracers, vertical_speed, diffusivity, buoyancy_force, wet_levels, surface_patch,
    prior_height, land_mask, baroclinic_map, barotropic_map,
):
    f32, i32 = jnp.float32, jnp.int32
    vmem = pl.BlockSpec(memory_space=pltpu.VMEM)
    hbm = pl.BlockSpec(memory_space=pltpu.HBM)
    tags = SUM_TAG + 1
    height_shape = (BLOCKS, BH, BW)
    tr, height = pl.pallas_call(
        step_kernel,
        out_shape=(pltpu.VMEM(tracers.shape, f32), pltpu.VMEM(height_shape, f32)),
        in_specs=[hbm] * 10,
        out_specs=(vmem, vmem),
        scratch_shapes=[
            pltpu.SMEM((NBY * GBX,), i32),
            pltpu.SMEM((NBY * GBX,), i32),
            pltpu.VMEM((LEV, BLOCKS, CELLS), jnp.bfloat16),
            pltpu.VMEM((BLOCKS, CELLS), i32),
            pltpu.VMEM((BLOCKS, CELLS), i32),
            pltpu.VMEM((BLOCKS, CELLS), f32),
            pltpu.VMEM(height_shape, i32),
            pltpu.VMEM((LEV, BLOCKS, CELLS), f32),
            pltpu.VMEM((LEV, BLOCKS, CELLS), f32),
            pltpu.VMEM((6, LEV, BLOCKS, 128), f32),
            pltpu.VMEM((4 * BLOCKS, 2, BH, BW), f32),
            pltpu.VMEM((4 * BLOCKS, 2, BH, BW), f32),
            pltpu.VMEM((3, 28, 8, BW), f32),
            pltpu.VMEM((4, 28, 8, BW), f32),
            pltpu.VMEM((2, 4, 18, 8, BW), f32),
            pltpu.VMEM((2, 4, 18, 8, BW), f32),
            pltpu.VMEM((BLOCKS, ITERS + 1, BH, BW), f32),
            pltpu.VMEM((ENTRIES, BW), f32),
            pltpu.VMEM((DEVICES, 1, BW), f32),
            pltpu.VMEM((8, BW), i32),
            pltpu.SMEM((8, BW), i32),
            pltpu.SemaphoreType.REGULAR,
            pltpu.SemaphoreType.REGULAR,
            pltpu.SemaphoreType.REGULAR,
            pltpu.SemaphoreType.DMA((10,)),
            pltpu.SemaphoreType.DMA((CHUNKS,)),
            pltpu.SemaphoreType.DMA((tags,)),
            pltpu.SemaphoreType.DMA((tags,)),
        ],
        compiler_params=pltpu.CompilerParams(
            collective_id=0, has_side_effects=True, vmem_limit_bytes=32 * 2**20
        ),
        name="step",
    )(
        *(
            pltpu.with_memory_space_constraint(array, pltpu.HBM)
            for array in (
                baroclinic_map, barotropic_map, buoyancy_force, wet_levels, surface_patch,
                prior_height, land_mask, vertical_speed, diffusivity, tracers,
            )
        )
    )
    return pl.pallas_call(
        write_kernel,
        out_shape=(
            jax.ShapeDtypeStruct(tracers.shape, f32), jax.ShapeDtypeStruct(height_shape, f32)
        ),
        in_specs=[vmem, vmem],
        out_specs=(hbm, hbm),
        scratch_shapes=[pltpu.SemaphoreType.DMA((CHUNKS + 1,))],
        compiler_params=pltpu.CompilerParams(vmem_limit_bytes=2 * 2**20),
        name="write",
    )(tr, height)


def solution(mesh):
    return jax.shard_map(
        local,
        mesh=mesh,
        in_specs=(
            P(None, ("by", "bx"), None, None),
            P(None, ("by", "bx"), None),
            P(None, ("by", "bx"), None),
            P(None, ("by", "bx"), None),
            P(("by", "bx"), None),
            P(("by", "bx"), None),
            P(("by", "bx"), None),
            P(("by", "bx"), None, None),
            P(),
            P(),
        ),
        out_specs=(P(None, ("by", "bx"), None, None), P(("by", "bx"), None, None)),
        check_vma=False,
    )
```
